128 devices in a mesh: ctx: 32 (over y, z, core), exp: 4 (over x).
Axes of the slice: x: 4, y: 4, z: 4, core: 2. Of those that a mesh axis runs over, the one named last changes fastest.
Arguments:
- inputs: bfloat16 [4096, 4096], P('ctx', 'exp'), may hold values from -6 to 6
- gate_input: bfloat16 [4096, 4096], P('ctx', 'exp')
- b_proj: bfloat16 [4096, 128], P('ctx'), may hold values from -0.5 to 0.5
- c_proj: bfloat16 [4096, 128], P('ctx'), may hold values from -6 to 6
- step_size: float32 [64, 4096], P('exp', 'ctx'), may hold values from 0.03 to 0.3
- decay_rate: float32 [64, 4096], P('exp', 'ctx'), as said below
- skip_gain: float32 [64], P('exp'), may hold values from 0.5 to 2
- start_state: float32 [64, 64, 128], P('exp'), may hold values from -3 to 3
- norm_gain: float32 [4096], P('exp'), may hold values from 0.5 to 1.5
- out_proj: bfloat16 [4096, 4096], P('exp', 'ctx'), may hold values from -0.09375 to 0.09375
- residual: bfloat16 [4096, 4096], P('ctx'), may hold values from -6 to 6
- moe_gain: float32 [4096], replicated, may hold values from 0.5 to 1.5
- w_gate: bfloat16 [32, 4096, 3584], P('ctx', None, 'exp'), may hold values from -0.09375 to 0.09375
- w_up: bfloat16 [32, 4096, 3584], P('ctx', None, 'exp'), may hold values from -0.09375 to 0.09375
- w_down: bfloat16 [32, 3584, 4096], P('ctx', 'exp'), may hold values from -0.0625 to 0.0625
- route_ids: int32 [4096, 2], P('ctx'), may hold values from 0 to 15, all different within a row; in each aligned block of 32 rows (0 to 31, 32 to 63, ...) at most 8 rows name the same one
- route_gates: float32 [4096, 2], P('ctx'), may hold values from 0.3 to 1
Outputs:
- output: bfloat16 [4096, 4096], P(('ctx', 'exp'))
The draws below stay inside these ranges and needn't reach their ends.
Inputs may be any that keep to these rules, and one draw needn't show every extreme that they name: `route_ids`: each row names two different experts. In each aligned block of 32 rows no expert is named more than 8 times, a bound that some block reaches. `decay_rate`: Non-negative.
All inputs are finite; a program needn't handle non-finite values.
Results may differ from the reference program's by a relative error of at most 0.02.
Values may be sent and summed in bfloat16 or wider, within the bound.
A program may use at most 128 MiB of HBM per device.

```python
import math
import jax
import jax.numpy as jnp
import numpy as np
from jax import lax

D = 4096
RECURRENT_GROUPS = 64
P_SIZE = 64
N = 128
FF = 7168
PAIR = 2
TOK_CTX = 128
EXPERTS = 16
SPAN_ENTRIES = 4096
TOK_Q = 32
CAP = 8
N_EXP = 4


def draw_gate_input(key, part):
    stochastic_seeds = jax.random.split(key, 3)
    columns = RECURRENT_GROUPS * P_SIZE
    ramp = jnp.exp(jnp.log(3.0) * jnp.arange(columns, dtype=jnp.float32) / columns)
    column_scale = ramp * jnp.exp(jax.random.uniform(stochastic_seeds[0], (columns,), minval=0.0, maxval=jnp.log(10.0))) / 3.0
    row_scale = jnp.exp(jax.random.uniform(stochastic_seeds[1], (SPAN_ENTRIES, 1), minval=0.0, maxval=jnp.log(4.0)))
    noise = jax.random.normal(stochastic_seeds[2], (SPAN_ENTRIES, columns))
    return (noise * row_scale * column_scale[None, :]).astype(jnp.bfloat16)


def draw_decay_rate(key, part):
    stochastic_seeds = jax.random.split(key, 7)
    fast_share = 0.5
    fast_heads = jax.random.uniform(stochastic_seeds[0], (RECURRENT_GROUPS,)) < fast_share
    fast_rate = jax.random.uniform(stochastic_seeds[1], (RECURRENT_GROUPS,), minval=1.0 / 50.0, maxval=1.0 / 30.0)
    slow_rate = jax.random.uniform(stochastic_seeds[2], (RECURRENT_GROUPS,), minval=0.1, maxval=0.5) / SPAN_ENTRIES
    nominal_speed = jnp.where(fast_heads, fast_rate, slow_rate)
    blocks = SPAN_ENTRIES // TOK_CTX
    hardware_multiplier = jnp.exp(jax.random.uniform(stochastic_seeds[3], (RECURRENT_GROUPS, blocks), minval=jnp.log(0.5), maxval=jnp.log(2.0)))
    hardware_multiplier = jnp.repeat(hardware_multiplier, TOK_CTX, axis=1)
    perturb_magnitude = jnp.exp(jax.random.uniform(stochastic_seeds[4], (RECURRENT_GROUPS, SPAN_ENTRIES), minval=jnp.log(0.7), maxval=jnp.log(1.4)))
    spike_offset = jax.random.randint(stochastic_seeds[5], (RECURRENT_GROUPS, 3), 0, SPAN_ENTRIES)
    spike_duration = jax.random.uniform(stochastic_seeds[6], (RECURRENT_GROUPS, 3), minval=0.22, maxval=0.5)
    sequence_indices = jnp.arange(SPAN_ENTRIES, dtype=jnp.int32)
    spike_collection = jnp.sum(jnp.where(sequence_indices[None, None, :] == spike_offset[:, :, None], spike_duration[:, :, None], 0.0), axis=1)
    return (nominal_speed[:, None] * hardware_multiplier * perturb_magnitude + spike_collection).astype(jnp.float32)


def block_scale(rng, shape, cuts, smallest, top_value):
    factor_of, own = 1.0, jax.random.fold_in(rng, 6)
    for dim, parts in cuts:
        heights = jnp.exp(jax.random.uniform(jax.random.fold_in(own, dim), (parts,), jnp.float32, smallest / len(cuts), top_value / len(cuts)))
        factor_of = factor_of * jnp.repeat(heights, shape[dim] // parts).reshape([-1 if axis == dim else 1 for axis in range(len(shape))])
    return factor_of


def shared_out(key, own, number, rows, amount, top, reach, skew):
    sequence = jax.random.permutation(key, amount)
    crowded, ordinary = portions_of(amount, rows * top, reach, skew, True), portions_of(amount, rows * top, reach, skew, False)
    places = jnp.arange(amount)

    def named(sizes, offset_by):
        used = int((sizes > 0).sum())
        fixed = max(1, used // 4)
        shifted = fixed + (places - fixed + offset_by * (used - fixed)) % max(1, amount - fixed)
        return jnp.zeros((amount,), jnp.int32).at[sequence[jnp.where(places < fixed, places, shifted)]].set(jnp.asarray(sizes, jnp.int32))

    sizes = jnp.where(number % 4 == 0, named(crowded, number // 4), named(ordinary, number - number // 4 - 1))
    mixed = jax.random.permutation(jax.random.fold_in(own, 3), amount)
    giver, sink = mixed[0:amount // 2 * 2:2], mixed[1:amount // 2 * 2:2]
    margin = jnp.minimum(sizes[giver] - 1, reach - sizes[sink]) // 2
    margin = jnp.where((giver == sequence[0]) | (sink == sequence[0]) | (sizes[sink] == 0), 0, jnp.maximum(margin, 0))
    shifted = jax.random.randint(jax.random.fold_in(own, 4), (amount // 2,), 0, 1 << 20) % (margin + 1)
    sizes = sizes.at[giver].add(-shifted).at[sink].add(shifted)
    labels = jnp.searchsorted(jnp.cumsum(sizes), jnp.arange(rows * top), side="right").astype(jnp.int32)
    listing = labels.reshape(top, rows).T
    listing = listing[jax.random.permutation(jax.random.fold_in(own, 1), rows)]
    offset_by = jax.random.randint(jax.random.fold_in(own, 2), (rows, 1), 0, top)
    return jnp.take_along_axis(listing, (jnp.arange(top)[None, :] + offset_by) % top, axis=1)


def portions_of(count, total, reach, slope, full):
    weights = [(1 << 20) // math.isqrt(grade ** slope) + 1 for grade in range(1, count + 1)]
    largest = reach if full else min(reach, max(-(-total // count), total * weights[0] // sum(weights)))
    least = 1 if total - largest >= count - 1 else 0
    given, spare = [largest] + [least] * (count - 1), total - largest - least * (count - 1)
    while spare > 0:
        free = [i for i in range(1, count) if given[i] < largest] or [i for i in range(1, count) if given[i] < reach]
        pool, remaining = sum([weights[i] for i in free]), spare
        for i in free:
            more = min(reach - given[i], max(1, remaining * weights[i] // pool), spare)
            given[i] = given[i] + more
            spare = spare - more
    return np.array(given)


def normal_values(key, shape, scale, most, shards=(), held_as=jnp.bfloat16):
    drawn = scale * jax.random.normal(key, shape, jnp.float32)
    if shards:
        drawn = drawn * block_scale(key, shape, shards, -0.22, 0.18)
    return jnp.clip(drawn, -most, most).astype(held_as)


def setup_inputs(seed: int = 0) -> dict:
    splits = jax.random.split(jax.random.key(seed), 18)
    inputs = normal_values(splits[0], (SPAN_ENTRIES, RECURRENT_GROUPS * P_SIZE), 1.0, 6.0, ((0, 32), (1, 4)))
    gate_input = draw_gate_input(jax.random.fold_in(splits[17], 71), 0)
    b_proj = normal_values(splits[2], (SPAN_ENTRIES, N), N ** -0.5, 0.5, ((0, 32),))
    c_proj = normal_values(splits[3], (SPAN_ENTRIES, N), 1.0, 6.0, ((0, 32),))
    step_size = jnp.clip(jnp.exp(math.log(0.3) - 2.3025852 * jax.random.uniform(splits[4], (RECURRENT_GROUPS, SPAN_ENTRIES), jnp.float32) ** block_scale(splits[4], (RECURRENT_GROUPS, SPAN_ENTRIES), ((0, 4), (1, 32)), -0.2, 0.2)), 0.03, 0.3)
    decay_rate = draw_decay_rate(jax.random.fold_in(splits[17], 71), 0)
    skip_gain = jnp.clip(0.5 + 1.5 * jax.random.uniform(splits[6], (RECURRENT_GROUPS,), jnp.float32) ** block_scale(splits[6], (RECURRENT_GROUPS,), ((0, 4),), -0.2, 0.2), 0.5, 2.0)
    start_state = normal_values(splits[7], (RECURRENT_GROUPS, P_SIZE, N), 0.5, 3.0, ((0, 4),), jnp.float32)
    norm_gain = jnp.clip(1.0 + 0.1 * jax.random.normal(splits[8], (RECURRENT_GROUPS * P_SIZE,), jnp.float32), 0.5, 1.5)
    out_proj = normal_values(splits[9], (RECURRENT_GROUPS * P_SIZE, D), (RECURRENT_GROUPS * P_SIZE) ** -0.5, 0.09375, ((0, 4), (1, 32)))
    residual = normal_values(splits[10], (SPAN_ENTRIES, D), 1.0, 6.0, ((0, 32),))
    moe_gain = jnp.clip(1.0 + 0.1 * jax.random.normal(splits[11], (D,), jnp.float32), 0.5, 1.5)
    w_gate = normal_values(splits[12], (EXPERTS * PAIR, D, FF // PAIR), D ** -0.5, 0.09375, ((0, 32), (2, 4)))
    w_up = normal_values(splits[13], (EXPERTS * PAIR, D, FF // PAIR), D ** -0.5, 0.09375, ((0, 32), (2, 4)))
    w_down = normal_values(splits[14], (EXPERTS * PAIR, FF // PAIR, D), FF ** -0.5, 0.0625, ((0, 32), (1, 4)))
    route_ids_keys = jax.random.split(jax.random.fold_in(splits[15], 1), SPAN_ENTRIES // TOK_Q)
    route_ids_turns = jax.random.permutation(jax.random.fold_in(splits[15], 3), SPAN_ENTRIES // TOK_Q)
    route_ids = jax.vmap(lambda own, number: shared_out(jax.random.fold_in(splits[15], 2), own, number, TOK_Q, EXPERTS, 2, CAP, 2))(route_ids_keys, route_ids_turns).reshape((SPAN_ENTRIES, 2))
    route_gates = jnp.clip(0.3 + 0.7 * jax.random.uniform(splits[16], (SPAN_ENTRIES, 2), jnp.float32) ** block_scale(splits[16], (SPAN_ENTRIES, 2), ((0, 32),), -0.2, 0.2), 0.3, 1.0)
    return dict(inputs=inputs, gate_input=gate_input, b_proj=b_proj, c_proj=c_proj, step_size=step_size, decay_rate=decay_rate, skip_gain=skip_gain, start_state=start_state, norm_gain=norm_gain, out_proj=out_proj, residual=residual, moe_gain=moe_gain, w_gate=w_gate, w_up=w_up, w_down=w_down, route_ids=route_ids, route_gates=route_gates)


eps_norm = 1e-05
top_precision = lax.Precision.HIGHEST

def span_scan(carry_state, pieces):
    x_block, b_block, c_block, step_block, rate_block = pieces
    length = x_block.shape[0]
    cumulative = jnp.cumsum(rate_block, axis=1)
    span_total = cumulative[:, -1]
    sequence_indices = jnp.arange(length, dtype=jnp.int32)
    causal = sequence_indices[:, None] >= sequence_indices[None, :]
    spread = jnp.where(causal[None], cumulative[:, :, None] - cumulative[:, None, :], 0.0)
    scores = jnp.dot(c_block, b_block.T, precision=top_precision)
    mixing = jnp.where(causal[None], jnp.exp(-spread), 0.0) * scores[None] * step_block[:, None, :]
    inside_part = jnp.einsum('hts,shp->thp', mixing, x_block, precision=top_precision)
    carried = jnp.einsum('hpn,tn->thp', carry_state, c_block, precision=top_precision) * jnp.exp(-cumulative).T[:, :, None]
    ending = jnp.exp(-(span_total[:, None] - cumulative)) * step_block
    local_state = jnp.einsum('hs,shp,sn->hpn', ending, x_block, b_block, precision=top_precision)
    new_state = jnp.exp(-span_total)[:, None, None] * carry_state + local_state
    return (new_state, inside_part + carried)

def experts_apply(moe_in, w_gate, w_up, w_down, route_ids, route_gates):
    flat_ids = route_ids.reshape(-1).astype(jnp.int32)
    rows_most = SPAN_ENTRIES // TOK_Q * CAP
    piece_width = FF // (PAIR * N_EXP)

    def one_expert(accumulated, expert):
        route_order = jnp.argsort((flat_ids != expert).astype(jnp.int32), stable=True)[:rows_most].astype(jnp.int32)
        is_live = flat_ids[route_order] == expert
        routed = moe_in[route_order // 2]
        result = jnp.zeros((rows_most, D), jnp.float32)
        for half_index in range(PAIR):
            row_index = (expert * PAIR + half_index).astype(jnp.int32)
            gate_part = lax.dynamic_index_in_dim(w_gate, row_index, 0, keepdims=False)
            up_part = lax.dynamic_index_in_dim(w_up, row_index, 0, keepdims=False)
            down_part = lax.dynamic_index_in_dim(w_down, row_index, 0, keepdims=False)
            half_sum = jnp.zeros((rows_most, D), jnp.float32)
            for quarter in range(N_EXP):
                lower = quarter * piece_width
                upper = lower + piece_width
                gate_val = jnp.dot(routed, gate_part[:, lower:upper], preferred_element_type=jnp.float32)
                up_val = jnp.dot(routed, up_part[:, lower:upper], preferred_element_type=jnp.float32)
                hidden_piece = (jax.nn.silu(gate_val) * up_val).astype(jnp.bfloat16)
                product = jnp.dot(hidden_piece, down_part[lower:upper, :], preferred_element_type=jnp.float32)
                half_sum = half_sum + lax.optimization_barrier(product.astype(jnp.bfloat16)).astype(jnp.float32)
            result = result + lax.optimization_barrier(half_sum.astype(jnp.bfloat16)).astype(jnp.float32)
        accumulated = accumulated.at[route_order].add(jnp.where(is_live[:, None], result, 0.0))
        return (accumulated, None)
    start_value = jnp.zeros((2 * SPAN_ENTRIES, D), jnp.float32)
    totals, unused = lax.scan(one_expert, start_value, jnp.arange(EXPERTS, dtype=jnp.int32))
    return lax.optimization_barrier(jnp.sum(totals.reshape(SPAN_ENTRIES, 2, D) * route_gates[:, :, None].astype(jnp.float32), axis=1))

def reference(inputs, gate_input, b_proj, c_proj, step_size, decay_rate, skip_gain, start_state, norm_gain, out_proj, residual, moe_gain, w_gate, w_up, w_down, route_ids, route_gates):
    spans = SPAN_ENTRIES // TOK_CTX
    x_whole = inputs.astype(jnp.float32)
    x_all = x_whole.reshape(spans, TOK_CTX, RECURRENT_GROUPS, P_SIZE)
    b_all = b_proj.astype(jnp.float32).reshape(spans, TOK_CTX, N)
    c_all = c_proj.astype(jnp.float32).reshape(spans, TOK_CTX, N)
    step_all = step_size.reshape(RECURRENT_GROUPS, spans, TOK_CTX).transpose(1, 0, 2)
    rate_all = decay_rate.reshape(RECURRENT_GROUPS, spans, TOK_CTX).transpose(1, 0, 2)
    end_state, ssm_part = lax.scan(span_scan, start_state.astype(jnp.float32), (x_all, b_all, c_all, step_all, rate_all))
    ssm_out = ssm_part.reshape(SPAN_ENTRIES, RECURRENT_GROUPS, P_SIZE) + skip_gain[None, :, None] * x_whole.reshape(SPAN_ENTRIES, RECURRENT_GROUPS, P_SIZE)
    gated_out = ssm_out.reshape(SPAN_ENTRIES, RECURRENT_GROUPS * P_SIZE) * jax.nn.silu(gate_input.astype(jnp.float32))
    scaling = lax.rsqrt(lax.optimization_barrier(jnp.mean(gated_out * gated_out, axis=1, keepdims=True)) + eps_norm)
    normed_mix = (gated_out * scaling * norm_gain[None, :]).astype(jnp.bfloat16)
    mixed = jnp.dot(normed_mix, out_proj, preferred_element_type=jnp.float32)
    hidden = residual.astype(jnp.float32) + mixed
    moe_scale = lax.rsqrt(lax.optimization_barrier(jnp.mean(hidden * hidden, axis=1, keepdims=True)) + eps_norm)
    moe_in = (hidden * moe_scale * moe_gain[None, :]).astype(jnp.bfloat16)
    moe_out = experts_apply(moe_in, w_gate, w_up, w_down, route_ids, route_gates)
    return (hidden + moe_out).astype(jnp.bfloat16)
```

```python
import jax
import jax.numpy as jnp
from jax import lax
from jax.sharding import PartitionSpec as P

PAIR = 2


eps_norm = 1e-05
top_precision = lax.Precision.HIGHEST


def entering(x, axis, join, neutral):
    place = lax.axis_index(axis)
    decay, state = x
    packed = jnp.concatenate(
        [state, jnp.broadcast_to(decay[:, None, None], (state.shape[0], 1, state.shape[2]))], axis=1
    )
    gathered = lax.all_gather(packed.astype(jnp.bfloat16), axis)
    start = jax.tree.map(lambda a, e: jnp.zeros_like(a) + jnp.asarray(e, a.dtype), x, neutral)

    def one(hop, carry):
        block = lax.dynamic_index_in_dim(gathered, hop, 0, False).astype(jnp.float32)
        return join(carry, (block[:, -1, 0], block[:, :-1, :]))

    return lax.fori_loop(0, place, one, start)


def later_state(earlier, later):
    first_decay, first_state = earlier
    second_decay, second_state = later
    return (first_decay * second_decay, second_decay[:, None, None] * first_state + second_state)


def route_ranks(quarter_ids, experts):
    flattened = quarter_ids.reshape(-1)
    onehot = (flattened[:, None] == jnp.arange(experts, dtype=jnp.int32)[None, :]).astype(jnp.int32)
    running = jnp.cumsum(onehot, axis=0)
    rank_ids = jnp.sum(onehot * running, axis=1) - 1
    return (flattened, rank_ids)


def place_rows(normed, quarter_ids, experts, capacity):
    flattened, rank_ids = route_ranks(quarter_ids, experts)
    slot_ids = rank_ids * experts + flattened
    matches = (
        jnp.arange(capacity * experts, dtype=jnp.int32)[:, None] == slot_ids[None, :]
    ).astype(jnp.bfloat16)
    doubled = jnp.repeat(normed, quarter_ids.shape[1], axis=0)
    placed = jnp.dot(matches, doubled, preferred_element_type=jnp.float32).astype(jnp.bfloat16)
    return placed.reshape(capacity, experts, normed.shape[1])


def rms_rows(values, gain_vec):
    scaling = lax.rsqrt(jnp.mean(values * values, axis=1, keepdims=True) + eps_norm)
    return (values * scaling * gain_vec[None, :]).astype(jnp.bfloat16)


def local(
    inputs,
    gate_input,
    b_proj,
    c_proj,
    step_size,
    decay_rate,
    skip_gain,
    start_state,
    norm_gain,
    out_proj,
    residual,
    moe_gain,
    w_gate,
    w_up,
    w_down,
    route_ids,
    route_gates,
):
    tok_ctx = inputs.shape[0]
    head_count = step_size.shape[0]
    head_dim = inputs.shape[1] // head_count
    model_width = residual.shape[1]
    n_ctx = lax.axis_size("ctx")
    n_exp = lax.axis_size("exp")
    experts = n_ctx // PAIR
    tok_quarter = tok_ctx // n_exp
    capacity = 4 * tok_quarter // experts
    x_local = inputs.astype(jnp.float32).reshape(tok_ctx, head_count, head_dim)
    b_local = b_proj.astype(jnp.float32)
    c_local = c_proj.astype(jnp.float32)
    cumulative = jnp.cumsum(decay_rate, axis=1)
    span_total = cumulative[:, -1]
    sequence_indices = jnp.arange(tok_ctx, dtype=jnp.int32)
    causal = sequence_indices[:, None] >= sequence_indices[None, :]
    spread = jnp.where(causal[None], cumulative[:, :, None] - cumulative[:, None, :], 0.0)
    scores = jnp.dot(c_local, b_local.T, precision=top_precision)
    mixing = jnp.where(causal[None], jnp.exp(-spread), 0.0) * scores[None] * step_size[:, None, :]
    inside_part = jnp.einsum("hts,shp->thp", mixing, x_local, precision=top_precision)
    ending = jnp.exp(-(span_total[:, None] - cumulative)) * step_size
    local_state = jnp.einsum("hs,shp,sn->hpn", ending, x_local, b_local, precision=top_precision)
    prior_decay, prior_state = entering(
        (jnp.exp(-span_total), local_state),
        "ctx",
        later_state,
        (jnp.ones_like(span_total), jnp.zeros_like(local_state)),
    )
    incoming = prior_state + prior_decay[:, None, None] * start_state
    carried = (
        jnp.einsum("hpn,tn->thp", incoming, c_local, precision=top_precision)
        * jnp.exp(-cumulative).T[:, :, None]
    )
    ssm_out = inside_part + carried + skip_gain[None, :, None] * x_local
    gated_out = ssm_out.reshape(tok_ctx, head_count * head_dim) * jax.nn.silu(
        gate_input.astype(jnp.float32)
    )
    squares = lax.psum(jnp.sum(gated_out * gated_out, axis=1), "exp")
    scaling = lax.rsqrt(squares / (head_count * head_dim * n_exp) + eps_norm)
    normed_mix = (gated_out * scaling[:, None] * norm_gain[None, :]).astype(jnp.bfloat16)
    partial_value = jnp.dot(
        normed_mix,
        lax.all_gather(out_proj, "ctx", axis=1, tiled=True),
        preferred_element_type=jnp.float32,
    )
    gate_rows = w_gate[0]
    up_rows = w_up[0]
    down_rows = w_down[0]
    piece_width = gate_rows.shape[1]
    first_row = lax.axis_index("exp") * tok_quarter
    own_ids = lax.dynamic_slice_in_dim(route_ids, first_row, tok_quarter, 0)
    own_gates = lax.dynamic_slice_in_dim(route_gates, first_row, tok_quarter, 0)
    mixed_all = lax.psum(partial_value.astype(jnp.bfloat16), "exp").astype(jnp.float32)
    hidden_all = residual.astype(jnp.float32) + mixed_all
    moe_all = rms_rows(hidden_all, moe_gain)

    def place_quarter(quarter_rows, quarter_ids):
        return place_rows(quarter_rows, quarter_ids, experts, capacity)

    placed = jax.vmap(place_quarter)(
        moe_all.reshape(n_exp, tok_quarter, model_width),
        route_ids.reshape(n_exp, tok_quarter, route_ids.shape[1]),
    )
    placed = placed.reshape(n_exp * capacity, experts, model_width)
    outgoing = jnp.repeat(placed, PAIR, axis=1)
    arrived = lax.all_to_all(outgoing, "ctx", split_axis=1, concat_axis=1, tiled=True)
    flattened = arrived.reshape(-1, model_width)
    gate_val = jnp.dot(flattened, gate_rows, preferred_element_type=jnp.float32)
    up_val = jnp.dot(flattened, up_rows, preferred_element_type=jnp.float32)
    activated = (jax.nn.silu(gate_val) * up_val).astype(jnp.bfloat16)
    hidden = activated.reshape(arrived.shape[0], arrived.shape[1], piece_width)
    hidden_own = lax.dynamic_slice_in_dim(hidden_all, first_row, tok_quarter, 0)
    product = jnp.dot(
        hidden.reshape(-1, piece_width), down_rows, preferred_element_type=jnp.float32
    )
    rounded = lax.optimization_barrier(product.astype(jnp.bfloat16)).astype(jnp.float32)
    summed = lax.psum_scatter(
        rounded.reshape(lax.axis_size("exp") * capacity, hidden.shape[1], model_width).astype(
            jnp.bfloat16
        ),
        "exp",
        scatter_dimension=0,
        tiled=True,
    )
    halves = lax.all_to_all(summed, "ctx", split_axis=1, concat_axis=1, tiled=True)
    flattened, rank_ids = route_ranks(own_ids, experts)
    base_rows = rank_ids * n_ctx + flattened * PAIR
    fetch_rows = base_rows[:, None] + jnp.arange(PAIR, dtype=jnp.int32)[None, :]
    fetched = halves.reshape(capacity * n_ctx, model_width)[fetch_rows]
    expert_out = jnp.sum(fetched.astype(jnp.float32), axis=1)
    weighted = expert_out * own_gates.reshape(-1)[:, None]
    moe_out = jnp.sum(weighted.reshape(tok_quarter, -1, model_width), axis=1)
    return (hidden_own + moe_out).astype(jnp.bfloat16)


def solution(mesh):
    in_specs = (
        P("ctx", "exp"),
        P("ctx", "exp"),
        P("ctx", None),
        P("ctx", None),
        P("exp", "ctx"),
        P("exp", "ctx"),
        P("exp"),
        P("exp", None, None),
        P("exp"),
        P("exp", "ctx"),
        P("ctx", None),
        P(),
        P("ctx", None, "exp"),
        P("ctx", None, "exp"),
        P("ctx", "exp", None),
        P("ctx", None),
        P("ctx", None),
    )
    out_specs = P(("ctx", "exp"), None)
    return jax.shard_map(local, mesh=mesh, in_specs=in_specs, out_specs=out_specs, check_vma=False)
```

```python
import jax
import jax.numpy as jnp
from jax import lax
from jax.sharding import PartitionSpec as P

PAIR = 2


eps_norm = 1e-05
top_precision = lax.Precision.HIGHEST


def entering(decay, state, axis):
    place = lax.axis_index(axis)
    heads, rows, width = state.shape
    packed = jnp.concatenate(
        [state.reshape(heads, rows * width), jnp.broadcast_to(decay[:, None], (heads, width))], axis=1
    )
    gathered = lax.all_gather(packed.astype(jnp.bfloat16), axis)
    decays = gathered[:, :, rows * width].astype(jnp.float32)
    states = gathered[:, :, : rows * width]
    order = jnp.arange(gathered.shape[0], dtype=jnp.int32)
    earlier = order < place
    between = (order[None, :] > order[:, None]) & earlier[None, :]
    weights = jnp.prod(jnp.where(between[:, :, None], decays[None, :, :], 1.0), axis=1)
    weights = jnp.where(earlier[:, None], weights, 0.0)
    prior_decay = jnp.prod(jnp.where(earlier[:, None], decays, 1.0), axis=0)
    prior_state = jnp.sum(weights[:, :, None] * states.astype(jnp.float32), axis=0)
    return prior_decay, prior_state.reshape(heads, rows, width)


def route_ranks(quarter_ids, experts):
    flattened = quarter_ids.reshape(-1)
    onehot = (flattened[:, None] == jnp.arange(experts, dtype=jnp.int32)[None, :]).astype(jnp.int32)
    running = jnp.cumsum(onehot, axis=0)
    rank_ids = jnp.sum(onehot * running, axis=1) - 1
    return (flattened, rank_ids)


def place_rows(normed, quarter_ids, experts, capacity):
    flattened, rank_ids = route_ranks(quarter_ids, experts)
    slot_ids = rank_ids * experts + flattened
    matches = (
        jnp.arange(capacity * experts, dtype=jnp.int32)[:, None] == slot_ids[None, :]
    ).astype(jnp.bfloat16)
    doubled = jnp.repeat(normed, quarter_ids.shape[1], axis=0)
    placed = jnp.dot(matches, doubled, preferred_element_type=jnp.float32).astype(jnp.bfloat16)
    return placed.reshape(capacity, experts, normed.shape[1])


def rms_rows(values, gain_vec):
    scaling = lax.rsqrt(jnp.mean(values * values, axis=1, keepdims=True) + eps_norm)
    return (values * scaling * gain_vec[None, :]).astype(jnp.bfloat16)


def local(
    inputs,
    gate_input,
    b_proj,
    c_proj,
    step_size,
    decay_rate,
    skip_gain,
    start_state,
    norm_gain,
    out_proj,
    residual,
    moe_gain,
    w_gate,
    w_up,
    w_down,
    route_ids,
    route_gates,
):
    tok_ctx = inputs.shape[0]
    head_count = step_size.shape[0]
    head_dim = inputs.shape[1] // head_count
    model_width = residual.shape[1]
    n_ctx = lax.axis_size("ctx")
    n_exp = lax.axis_size("exp")
    experts = n_ctx // PAIR
    tok_quarter = tok_ctx // n_exp
    capacity = 4 * tok_quarter // experts
    x_local = inputs.astype(jnp.float32).reshape(tok_ctx, head_count, head_dim)
    b_local = b_proj.astype(jnp.float32)
    c_local = c_proj.astype(jnp.float32)
    cumulative = jnp.cumsum(decay_rate, axis=1)
    span_total = cumulative[:, -1]
    sequence_indices = jnp.arange(tok_ctx, dtype=jnp.int32)
    causal = sequence_indices[:, None] >= sequence_indices[None, :]
    spread = jnp.where(causal[None], cumulative[:, :, None] - cumulative[:, None, :], 0.0)
    scores = jnp.dot(c_local, b_local.T, precision=top_precision)
    mixing = jnp.where(causal[None], jnp.exp(-spread), 0.0) * scores[None] * step_size[:, None, :]
    inside_part = jnp.einsum("hts,shp->thp", mixing, x_local, precision=top_precision)
    ending = jnp.exp(-(span_total[:, None] - cumulative)) * step_size
    local_state = jnp.einsum("hs,shp,sn->hpn", ending, x_local, b_local, precision=top_precision)
    prior_decay, prior_state = entering(jnp.exp(-span_total), local_state, "ctx")
    incoming = prior_state + prior_decay[:, None, None] * start_state
    carried = (
        jnp.einsum("hpn,tn->thp", incoming, c_local, precision=top_precision)
        * jnp.exp(-cumulative).T[:, :, None]
    )
    ssm_out = inside_part + carried + skip_gain[None, :, None] * x_local
    gated_out = ssm_out.reshape(tok_ctx, head_count * head_dim) * jax.nn.silu(
        gate_input.astype(jnp.float32)
    )
    squares = lax.psum(jnp.sum(gated_out * gated_out, axis=1), "exp")
    scaling = lax.rsqrt(squares / (head_count * head_dim * n_exp) + eps_norm)
    normed_mix = (gated_out * scaling[:, None] * norm_gain[None, :]).astype(jnp.bfloat16)
    partial_value = jnp.dot(
        normed_mix,
        lax.all_gather(out_proj, "ctx", axis=1, tiled=True),
        preferred_element_type=jnp.float32,
    )
    gate_rows = w_gate[0]
    up_rows = w_up[0]
    down_rows = w_down[0]
    piece_width = gate_rows.shape[1]
    first_row = lax.axis_index("exp") * tok_quarter
    own_ids = lax.dynamic_slice_in_dim(route_ids, first_row, tok_quarter, 0)
    own_gates = lax.dynamic_slice_in_dim(route_gates, first_row, tok_quarter, 0)
    mixed_all = lax.psum(partial_value.astype(jnp.bfloat16), "exp").astype(jnp.float32)
    hidden_all = residual.astype(jnp.float32) + mixed_all
    moe_all = rms_rows(hidden_all, moe_gain)

    def place_quarter(quarter_rows, quarter_ids):
        return place_rows(quarter_rows, quarter_ids, experts, capacity)

    placed = jax.vmap(place_quarter)(
        moe_all.reshape(n_exp, tok_quarter, model_width),
        route_ids.reshape(n_exp, tok_quarter, route_ids.shape[1]),
    )
    placed = placed.reshape(n_exp * capacity, experts, model_width)
    outgoing = jnp.repeat(placed, PAIR, axis=1)
    arrived = lax.all_to_all(outgoing, "ctx", split_axis=1, concat_axis=1, tiled=True)
    flattened = arrived.reshape(-1, model_width)
    gate_val = jnp.dot(flattened, gate_rows, preferred_element_type=jnp.float32)
    up_val = jnp.dot(flattened, up_rows, preferred_element_type=jnp.float32)
    activated = (jax.nn.silu(gate_val) * up_val).astype(jnp.bfloat16)
    hidden = activated.reshape(arrived.shape[0], arrived.shape[1], piece_width)
    hidden_own = lax.dynamic_slice_in_dim(hidden_all, first_row, tok_quarter, 0)
    product = jnp.dot(
        hidden.reshape(-1, piece_width), down_rows, preferred_element_type=jnp.float32
    )
    rounded = lax.optimization_barrier(product.astype(jnp.bfloat16)).astype(jnp.float32)
    summed = lax.psum_scatter(
        rounded.reshape(lax.axis_size("exp") * capacity, hidden.shape[1], model_width).astype(
            jnp.bfloat16
        ),
        "exp",
        scatter_dimension=0,
        tiled=True,
    )
    halves = lax.all_to_all(summed, "ctx", split_axis=1, concat_axis=1, tiled=True)
    flattened, rank_ids = route_ranks(own_ids, experts)
    base_rows = rank_ids * n_ctx + flattened * PAIR
    fetch_rows = base_rows[:, None] + jnp.arange(PAIR, dtype=jnp.int32)[None, :]
    fetched = halves.reshape(capacity * n_ctx, model_width)[fetch_rows]
    expert_out = jnp.sum(fetched.astype(jnp.float32), axis=1)
    weighted = expert_out * own_gates.reshape(-1)[:, None]
    moe_out = jnp.sum(weighted.reshape(tok_quarter, -1, model_width), axis=1)
    return (hidden_own + moe_out).astype(jnp.bfloat16)


def solution(mesh):
    in_specs = (
        P("ctx", "exp"),
        P("ctx", "exp"),
        P("ctx", None),
        P("ctx", None),
        P("exp", "ctx"),
        P("exp", "ctx"),
        P("exp"),
        P("exp", None, None),
        P("exp"),
        P("exp", "ctx"),
        P("ctx", None),
        P(),
        P("ctx", None, "exp"),
        P("ctx", None, "exp"),
        P("ctx", "exp", None),
        P("ctx", None),
        P("ctx", None),
    )
    out_specs = P(("ctx", "exp"), None)
    return jax.shard_map(local, mesh=mesh, in_specs=in_specs, out_specs=out_specs, check_vma=False)
```

```python
import jax
import jax.numpy as jnp
from jax import lax
from jax.sharding import PartitionSpec as P

PAIR = 2


eps_norm = 1e-05
top_precision = lax.Precision.HIGHEST


def combine(earlier, later):
    first_decay, first_state = earlier
    second_decay, second_state = later
    return (first_decay * second_decay, second_decay[:, None, None] * first_state + second_state)


def entering(decay, state, axis):
    place = lax.axis_index(axis)
    count = lax.axis_size(axis)
    heads, rows, width = state.shape
    inclusive = (decay, state)
    exclusive = (jnp.ones_like(decay), jnp.zeros_like(state))
    hop = 1
    while hop < count:
        packed = jnp.concatenate(
            [inclusive[1].reshape(heads, rows * width), jnp.broadcast_to(inclusive[0][:, None], (heads, width))],
            axis=1,
        ).astype(jnp.bfloat16)
        got = lax.ppermute(packed, axis, [(i, i + hop) for i in range(count - hop)]).astype(jnp.float32)
        valid = place >= hop
        arrived = (
            jnp.where(valid, got[:, rows * width], 1.0),
            jnp.where(valid, got[:, : rows * width], 0.0).reshape(heads, rows, width),
        )
        inclusive = combine(arrived, inclusive)
        exclusive = combine(arrived, exclusive)
        hop *= 2
    return exclusive


def route_ranks(quarter_ids, experts):
    flattened = quarter_ids.reshape(-1)
    onehot = (flattened[:, None] == jnp.arange(experts, dtype=jnp.int32)[None, :]).astype(jnp.int32)
    running = jnp.cumsum(onehot, axis=0)
    rank_ids = jnp.sum(onehot * running, axis=1) - 1
    return (flattened, rank_ids)


def place_rows(normed, quarter_ids, experts, capacity):
    flattened, rank_ids = route_ranks(quarter_ids, experts)
    slot_ids = rank_ids * experts + flattened
    matches = (
        jnp.arange(capacity * experts, dtype=jnp.int32)[:, None] == slot_ids[None, :]
    ).astype(jnp.bfloat16)
    doubled = jnp.repeat(normed, quarter_ids.shape[1], axis=0)
    placed = jnp.dot(matches, doubled, preferred_element_type=jnp.float32).astype(jnp.bfloat16)
    return placed.reshape(capacity, experts, normed.shape[1])


def rms_rows(values, gain_vec):
    scaling = lax.rsqrt(jnp.mean(values * values, axis=1, keepdims=True) + eps_norm)
    return (values * scaling * gain_vec[None, :]).astype(jnp.bfloat16)


def local(
    inputs,
    gate_input,
    b_proj,
    c_proj,
    step_size,
    decay_rate,
    skip_gain,
    start_state,
    norm_gain,
    out_proj,
    residual,
    moe_gain,
    w_gate,
    w_up,
    w_down,
    route_ids,
    route_gates,
):
    tok_ctx = inputs.shape[0]
    head_count = step_size.shape[0]
    head_dim = inputs.shape[1] // head_count
    model_width = residual.shape[1]
    n_ctx = lax.axis_size("ctx")
    n_exp = lax.axis_size("exp")
    experts = n_ctx // PAIR
    tok_quarter = tok_ctx // n_exp
    capacity = 4 * tok_quarter // experts
    x_local = inputs.astype(jnp.float32).reshape(tok_ctx, head_count, head_dim)
    b_local = b_proj.astype(jnp.float32)
    c_local = c_proj.astype(jnp.float32)
    cumulative = jnp.cumsum(decay_rate, axis=1)
    span_total = cumulative[:, -1]
    sequence_indices = jnp.arange(tok_ctx, dtype=jnp.int32)
    causal = sequence_indices[:, None] >= sequence_indices[None, :]
    spread = jnp.where(causal[None], cumulative[:, :, None] - cumulative[:, None, :], 0.0)
    scores = jnp.dot(c_local, b_local.T, precision=top_precision)
    mixing = jnp.where(causal[None], jnp.exp(-spread), 0.0) * scores[None] * step_size[:, None, :]
    inside_part = jnp.einsum("hts,shp->thp", mixing, x_local, precision=top_precision)
    ending = jnp.exp(-(span_total[:, None] - cumulative)) * step_size
    local_state = jnp.einsum("hs,shp,sn->hpn", ending, x_local, b_local, precision=top_precision)
    prior_decay, prior_state = entering(jnp.exp(-span_total), local_state, "ctx")
    incoming = prior_state + prior_decay[:, None, None] * start_state
    carried = (
        jnp.einsum("hpn,tn->thp", incoming, c_local, precision=top_precision)
        * jnp.exp(-cumulative).T[:, :, None]
    )
    ssm_out = inside_part + carried + skip_gain[None, :, None] * x_local
    gated_out = ssm_out.reshape(tok_ctx, head_count * head_dim) * jax.nn.silu(
        gate_input.astype(jnp.float32)
    )
    squares = jnp.sum(gated_out * gated_out, axis=1)
    unscaled_mix = (gated_out * norm_gain[None, :]).astype(jnp.bfloat16)
    partial_value = jnp.dot(
        unscaled_mix,
        lax.all_gather(out_proj, "ctx", axis=1, tiled=True),
        preferred_element_type=jnp.float32,
    )
    width_out = partial_value.shape[1]
    summed_parts = lax.psum(
        jnp.concatenate(
            [partial_value, jnp.broadcast_to(squares[:, None], (tok_ctx, 128))], axis=1
        ).astype(jnp.bfloat16),
        "exp",
    ).astype(jnp.float32)
    scaling = lax.rsqrt(summed_parts[:, width_out] / (head_count * head_dim * n_exp) + eps_norm)
    mixed_all = summed_parts[:, :width_out] * scaling[:, None]
    gate_rows = w_gate[0]
    up_rows = w_up[0]
    down_rows = w_down[0]
    piece_width = gate_rows.shape[1]
    first_row = lax.axis_index("exp") * tok_quarter
    own_ids = lax.dynamic_slice_in_dim(route_ids, first_row, tok_quarter, 0)
    own_gates = lax.dynamic_slice_in_dim(route_gates, first_row, tok_quarter, 0)
    hidden_all = residual.astype(jnp.float32) + mixed_all
    moe_all = rms_rows(hidden_all, moe_gain)

    def place_quarter(quarter_rows, quarter_ids):
        return place_rows(quarter_rows, quarter_ids, experts, capacity)

    placed = jax.vmap(place_quarter)(
        moe_all.reshape(n_exp, tok_quarter, model_width),
        route_ids.reshape(n_exp, tok_quarter, route_ids.shape[1]),
    )
    placed = placed.reshape(n_exp * capacity, experts, model_width)
    outgoing = jnp.repeat(placed, PAIR, axis=1)
    arrived = lax.all_to_all(outgoing, "ctx", split_axis=1, concat_axis=1, tiled=True)
    flattened = arrived.reshape(-1, model_width)
    gate_val = jnp.dot(flattened, gate_rows, preferred_element_type=jnp.float32)
    up_val = jnp.dot(flattened, up_rows, preferred_element_type=jnp.float32)
    activated = (jax.nn.silu(gate_val) * up_val).astype(jnp.bfloat16)
    hidden = activated.reshape(arrived.shape[0], arrived.shape[1], piece_width)
    hidden_own = lax.dynamic_slice_in_dim(hidden_all, first_row, tok_quarter, 0)
    product = jnp.dot(
        hidden.reshape(-1, piece_width), down_rows, preferred_element_type=jnp.float32
    )
    rounded = lax.optimization_barrier(product.astype(jnp.bfloat16)).astype(jnp.float32)
    summed = lax.psum_scatter(
        rounded.reshape(lax.axis_size("exp") * capacity, hidden.shape[1], model_width).astype(
            jnp.bfloat16
        ),
        "exp",
        scatter_dimension=0,
        tiled=True,
    )
    halves = lax.all_to_all(summed, "ctx", split_axis=1, concat_axis=1, tiled=True)
    flattened, rank_ids = route_ranks(own_ids, experts)
    base_rows = rank_ids * n_ctx + flattened * PAIR
    fetch_rows = base_rows[:, None] + jnp.arange(PAIR, dtype=jnp.int32)[None, :]
    fetched = halves.reshape(capacity * n_ctx, model_width)[fetch_rows]
    expert_out = jnp.sum(fetched.astype(jnp.float32), axis=1)
    weighted = expert_out * own_gates.reshape(-1)[:, None]
    moe_out = jnp.sum(weighted.reshape(tok_quarter, -1, model_width), axis=1)
    return (hidden_own + moe_out).astype(jnp.bfloat16)


def solution(mesh):
    in_specs = (
        P("ctx", "exp"),
        P("ctx", "exp"),
        P("ctx", None),
        P("ctx", None),
        P("exp", "ctx"),
        P("exp", "ctx"),
        P("exp"),
        P("exp", None, None),
        P("exp"),
        P("exp", "ctx"),
        P("ctx", None),
        P(),
        P("ctx", None, "exp"),
        P("ctx", None, "exp"),
        P("ctx", "exp", None),
        P("ctx", None),
        P("ctx", None),
    )
    out_specs = P(("ctx", "exp"), None)
    return jax.shard_map(local, mesh=mesh, in_specs=in_specs, out_specs=out_specs, check_vma=False)
```

```python
import jax
import jax.numpy as jnp
from jax import lax
from jax.sharding import Mesh, PartitionSpec as P

PAIR = 2
CTX = ("chip", "core")


eps_norm = 1e-05
top_precision = lax.Precision.HIGHEST


def combine(earlier, later):
    first_decay, first_state = earlier
    second_decay, second_state = later
    return (first_decay * second_decay, second_decay[:, None, None] * first_state + second_state)


def entering(decay, state, axis):
    place = lax.axis_index("chip") * lax.axis_size("core") + lax.axis_index("core")
    count = lax.axis_size("chip") * lax.axis_size("core")
    heads, rows, width = state.shape
    inclusive = (decay, state)
    exclusive = (jnp.ones_like(decay), jnp.zeros_like(state))
    hop = 1
    while hop < count:
        packed = jnp.concatenate(
            [inclusive[1].reshape(heads, rows * width), jnp.broadcast_to(inclusive[0][:, None], (heads, width))],
            axis=1,
        ).astype(jnp.bfloat16)
        got = lax.ppermute(packed, axis, [(i, i + hop) for i in range(count - hop)]).astype(jnp.float32)
        valid = place >= hop
        arrived = (
            jnp.where(valid, got[:, rows * width], 1.0),
            jnp.where(valid, got[:, : rows * width], 0.0).reshape(heads, rows, width),
        )
        inclusive = combine(arrived, inclusive)
        exclusive = combine(arrived, exclusive)
        hop *= 2
    return exclusive


def route_ranks(quarter_ids, experts):
    flattened = quarter_ids.reshape(-1)
    onehot = (flattened[:, None] == jnp.arange(experts, dtype=jnp.int32)[None, :]).astype(jnp.int32)
    running = jnp.cumsum(onehot, axis=0)
    rank_ids = jnp.sum(onehot * running, axis=1) - 1
    return (flattened, rank_ids)


def place_rows(normed, quarter_ids, experts, capacity):
    flattened, rank_ids = route_ranks(quarter_ids, experts)
    slot_ids = rank_ids * experts + flattened
    matches = (
        jnp.arange(capacity * experts, dtype=jnp.int32)[:, None] == slot_ids[None, :]
    ).astype(jnp.bfloat16)
    doubled = jnp.repeat(normed, quarter_ids.shape[1], axis=0)
    placed = jnp.dot(matches, doubled, preferred_element_type=jnp.float32).astype(jnp.bfloat16)
    return placed.reshape(capacity, experts, normed.shape[1])


def rms_rows(values, gain_vec):
    scaling = lax.rsqrt(jnp.mean(values * values, axis=1, keepdims=True) + eps_norm)
    return (values * scaling * gain_vec[None, :]).astype(jnp.bfloat16)


def local(
    inputs,
    gate_input,
    b_proj,
    c_proj,
    step_size,
    decay_rate,
    skip_gain,
    start_state,
    norm_gain,
    out_proj,
    residual,
    moe_gain,
    w_gate,
    w_up,
    w_down,
    route_ids,
    route_gates,
):
    tok_ctx = inputs.shape[0]
    head_count = step_size.shape[0]
    head_dim = inputs.shape[1] // head_count
    model_width = residual.shape[1]
    n_ctx = lax.axis_size("chip") * lax.axis_size("core")
    n_exp = lax.axis_size("exp")
    experts = n_ctx // PAIR
    tok_quarter = tok_ctx // n_exp
    capacity = 4 * tok_quarter // experts
    x_local = inputs.astype(jnp.float32).reshape(tok_ctx, head_count, head_dim)
    b_local = b_proj.astype(jnp.float32)
    c_local = c_proj.astype(jnp.float32)
    cumulative = jnp.cumsum(decay_rate, axis=1)
    span_total = cumulative[:, -1]
    sequence_indices = jnp.arange(tok_ctx, dtype=jnp.int32)
    causal = sequence_indices[:, None] >= sequence_indices[None, :]
    spread = jnp.where(causal[None], cumulative[:, :, None] - cumulative[:, None, :], 0.0)
    scores = jnp.dot(c_local, b_local.T, precision=top_precision)
    mixing = jnp.where(causal[None], jnp.exp(-spread), 0.0) * scores[None] * step_size[:, None, :]
    inside_part = jnp.einsum("hts,shp->thp", mixing, x_local, precision=top_precision)
    ending = jnp.exp(-(span_total[:, None] - cumulative)) * step_size
    local_state = jnp.einsum("hs,shp,sn->hpn", ending, x_local, b_local, precision=top_precision)
    prior_decay, prior_state = entering(jnp.exp(-span_total), local_state, CTX)
    incoming = prior_state + prior_decay[:, None, None] * start_state
    carried = (
        jnp.einsum("hpn,tn->thp", incoming, c_local, precision=top_precision)
        * jnp.exp(-cumulative).T[:, :, None]
    )
    ssm_out = inside_part + carried + skip_gain[None, :, None] * x_local
    gated_out = ssm_out.reshape(tok_ctx, head_count * head_dim) * jax.nn.silu(
        gate_input.astype(jnp.float32)
    )
    squares = jnp.sum(gated_out * gated_out, axis=1)
    unscaled_mix = (gated_out * norm_gain[None, :]).astype(jnp.bfloat16)
    partial_value = jnp.dot(
        unscaled_mix,
        lax.all_gather(out_proj, CTX, axis=1, tiled=True),
        preferred_element_type=jnp.float32,
    )
    width_out = partial_value.shape[1]
    summed_parts = lax.psum(
        jnp.concatenate(
            [partial_value, jnp.broadcast_to(squares[:, None], (tok_ctx, 128))], axis=1
        ).astype(jnp.bfloat16),
        "exp",
    ).astype(jnp.float32)
    scaling = lax.rsqrt(summed_parts[:, width_out] / (head_count * head_dim * n_exp) + eps_norm)
    mixed_all = summed_parts[:, :width_out] * scaling[:, None]
    gate_rows = w_gate[0]
    up_rows = w_up[0]
    down_rows = w_down[0]
    piece_width = gate_rows.shape[1]
    first_row = lax.axis_index("exp") * tok_quarter
    own_ids = lax.dynamic_slice_in_dim(route_ids, first_row, tok_quarter, 0)
    own_gates = lax.dynamic_slice_in_dim(route_gates, first_row, tok_quarter, 0)
    hidden_all = residual.astype(jnp.float32) + mixed_all
    moe_all = rms_rows(hidden_all, moe_gain)

    def place_quarter(quarter_rows, quarter_ids):
        return place_rows(quarter_rows, quarter_ids, experts, capacity)

    placed = jax.vmap(place_quarter)(
        moe_all.reshape(n_exp, tok_quarter, model_width),
        route_ids.reshape(n_exp, tok_quarter, route_ids.shape[1]),
    )
    placed = placed.reshape(n_exp * capacity, experts, model_width)
    swap = [(0, 1), (1, 0)]
    mine = lax.all_to_all(placed, "chip", split_axis=1, concat_axis=1, tiled=True)
    other = lax.ppermute(mine, "core", swap)
    arrived = jnp.stack([mine, other], axis=1)
    flattened = arrived.reshape(-1, model_width)
    gate_val = jnp.dot(flattened, gate_rows, preferred_element_type=jnp.float32)
    up_val = jnp.dot(flattened, up_rows, preferred_element_type=jnp.float32)
    activated = (jax.nn.silu(gate_val) * up_val).astype(jnp.bfloat16)
    hidden_own = lax.dynamic_slice_in_dim(hidden_all, first_row, tok_quarter, 0)
    product = jnp.dot(activated, down_rows, preferred_element_type=jnp.float32)
    rounded = lax.optimization_barrier(product.astype(jnp.bfloat16))
    summed = lax.psum_scatter(
        rounded.reshape(arrived.shape), "exp", scatter_dimension=0, tiled=True
    )
    partner_half = lax.ppermute(summed[:, 1], "core", swap)
    both_halves = (summed[:, 0].astype(jnp.float32) + partner_half.astype(jnp.float32)).astype(jnp.bfloat16)
    returned = lax.all_to_all(both_halves, "chip", split_axis=1, concat_axis=1, tiled=True)
    flattened, rank_ids = route_ranks(own_ids, experts)
    fetched = returned.reshape(capacity * experts, model_width)[rank_ids * experts + flattened]
    weighted = fetched.astype(jnp.float32) * own_gates.reshape(-1)[:, None]
    moe_out = jnp.sum(weighted.reshape(tok_quarter, -1, model_width), axis=1)
    return (hidden_own + moe_out).astype(jnp.bfloat16)


def solution(mesh):
    in_specs = (
        P(CTX, "exp"),
        P(CTX, "exp"),
        P(CTX, None),
        P(CTX, None),
        P("exp", CTX),
        P("exp", CTX),
        P("exp"),
        P("exp", None, None),
        P("exp"),
        P("exp", CTX),
        P(CTX, None),
        P(),
        P(CTX, None, "exp"),
        P(CTX, None, "exp"),
        P(CTX, "exp", None),
        P(CTX, None),
        P(CTX, None),
    )
    out_specs = P(("chip", "core", "exp"), None)
    split_mesh = Mesh(
        mesh.devices.reshape(mesh.devices.shape[0] // 2, 2, mesh.devices.shape[1]), ("chip", "core", "exp")
    )
    return jax.shard_map(local, mesh=split_mesh, in_specs=in_specs, out_specs=out_specs, check_vma=False)
```

```python
import jax
import jax.numpy as jnp
from jax import lax
from jax.sharding import Mesh, PartitionSpec as P

PAIR = 2
CTX = ("chip", "core")


eps_norm = 1e-05
top_precision = lax.Precision.HIGHEST


def combine(earlier, later):
    first_decay, first_state = earlier
    second_decay, second_state = later
    return (first_decay * second_decay, second_decay[:, None, None] * first_state + second_state)


def entering(decay, state, axis):
    place = lax.axis_index("chip") * lax.axis_size("core") + lax.axis_index("core")
    count = lax.axis_size("chip") * lax.axis_size("core")
    heads, rows, width = state.shape
    inclusive = (decay, state)
    exclusive = (jnp.ones_like(decay), jnp.zeros_like(state))
    hop = 1
    while hop < count:
        packed = jnp.concatenate(
            [inclusive[1].reshape(heads, rows * width), jnp.broadcast_to(inclusive[0][:, None], (heads, width))],
            axis=1,
        ).astype(jnp.bfloat16)
        got = lax.ppermute(packed, axis, [(i, i + hop) for i in range(count - hop)]).astype(jnp.float32)
        valid = place >= hop
        arrived = (
            jnp.where(valid, got[:, rows * width], 1.0),
            jnp.where(valid, got[:, : rows * width], 0.0).reshape(heads, rows, width),
        )
        inclusive = combine(arrived, inclusive)
        exclusive = combine(arrived, exclusive)
        hop *= 2
    return exclusive


def route_ranks(quarter_ids, experts):
    flattened = quarter_ids.reshape(-1)
    onehot = (flattened[:, None] == jnp.arange(experts, dtype=jnp.int32)[None, :]).astype(jnp.int32)
    running = jnp.cumsum(onehot, axis=0)
    rank_ids = jnp.sum(onehot * running, axis=1) - 1
    return (flattened, rank_ids)


def place_rows(normed, quarter_ids, experts, capacity):
    flattened, rank_ids = route_ranks(quarter_ids, experts)
    slot_ids = rank_ids * experts + flattened
    matches = (
        jnp.arange(capacity * experts, dtype=jnp.int32)[:, None] == slot_ids[None, :]
    ).astype(jnp.bfloat16)
    doubled = jnp.repeat(normed, quarter_ids.shape[1], axis=0)
    placed = jnp.dot(matches, doubled, preferred_element_type=jnp.float32).astype(jnp.bfloat16)
    return placed.reshape(capacity, experts, normed.shape[1])


def rms_rows(values, gain_vec):
    scaling = lax.rsqrt(jnp.mean(values * values, axis=1, keepdims=True) + eps_norm)
    return (values * scaling * gain_vec[None, :]).astype(jnp.bfloat16)


def local(
    inputs,
    gate_input,
    b_proj,
    c_proj,
    step_size,
    decay_rate,
    skip_gain,
    start_state,
    norm_gain,
    out_proj,
    residual,
    moe_gain,
    w_gate,
    w_up,
    w_down,
    route_ids,
    route_gates,
):
    tok_ctx = inputs.shape[0]
    head_count = step_size.shape[0]
    head_dim = inputs.shape[1] // head_count
    model_width = residual.shape[1]
    n_ctx = lax.axis_size("chip") * lax.axis_size("core")
    n_exp = lax.axis_size("exp")
    experts = n_ctx // PAIR
    tok_quarter = tok_ctx // n_exp
    capacity = 4 * tok_quarter // experts
    x_local = inputs.astype(jnp.float32).reshape(tok_ctx, head_count, head_dim)
    b_local = b_proj.astype(jnp.float32)
    c_local = c_proj.astype(jnp.float32)
    cumulative = jnp.cumsum(decay_rate, axis=1)
    span_total = cumulative[:, -1]
    sequence_indices = jnp.arange(tok_ctx, dtype=jnp.int32)
    causal = sequence_indices[:, None] >= sequence_indices[None, :]
    spread = jnp.where(causal[None], cumulative[:, :, None] - cumulative[:, None, :], 0.0)
    scores = jnp.dot(c_local, b_local.T, precision=top_precision)
    mixing = jnp.where(causal[None], jnp.exp(-spread), 0.0) * scores[None] * step_size[:, None, :]
    inside_part = jnp.einsum("hts,shp->thp", mixing, x_local, precision=top_precision)
    ending = jnp.exp(-(span_total[:, None] - cumulative)) * step_size
    local_state = jnp.einsum("hs,shp,sn->hpn", ending, x_local, b_local, precision=top_precision)
    prior_decay, prior_state = entering(jnp.exp(-span_total), local_state, CTX)
    incoming = prior_state + prior_decay[:, None, None] * start_state
    carried = (
        jnp.einsum("hpn,tn->thp", incoming, c_local, precision=top_precision)
        * jnp.exp(-cumulative).T[:, :, None]
    )
    ssm_out = inside_part + carried + skip_gain[None, :, None] * x_local
    gated_out = ssm_out.reshape(tok_ctx, head_count * head_dim) * jax.nn.silu(
        gate_input.astype(jnp.float32)
    )
    squares = jnp.sum(gated_out * gated_out, axis=1)
    unscaled_mix = (gated_out * norm_gain[None, :]).astype(jnp.bfloat16)
    partial_value = jnp.dot(
        unscaled_mix,
        lax.all_gather(out_proj, CTX, axis=1, tiled=True),
        preferred_element_type=jnp.float32,
    )
    width_out = partial_value.shape[1]
    summed_parts = lax.psum(
        jnp.concatenate(
            [partial_value, jnp.broadcast_to(squares[:, None], (tok_ctx, 128))], axis=1
        ).astype(jnp.bfloat16),
        "exp",
    ).astype(jnp.float32)
    scaling = lax.rsqrt(summed_parts[:, width_out] / (head_count * head_dim * n_exp) + eps_norm)
    mixed_all = summed_parts[:, :width_out] * scaling[:, None]
    gate_rows = w_gate[0]
    up_rows = w_up[0]
    down_rows = w_down[0]
    piece_width = gate_rows.shape[1]
    first_row = lax.axis_index("exp") * tok_quarter
    own_ids = lax.dynamic_slice_in_dim(route_ids, first_row, tok_quarter, 0)
    own_gates = lax.dynamic_slice_in_dim(route_gates, first_row, tok_quarter, 0)
    hidden_all = residual.astype(jnp.float32) + mixed_all
    moe_all = rms_rows(hidden_all, moe_gain)

    def place_quarter(quarter_rows, quarter_ids):
        return place_rows(quarter_rows, quarter_ids, experts, capacity)

    placed = jax.vmap(place_quarter)(
        moe_all.reshape(n_exp, tok_quarter, model_width),
        route_ids.reshape(n_exp, tok_quarter, route_ids.shape[1]),
    )
    placed = placed.reshape(n_exp * capacity, experts, model_width)
    swap = [(0, 1), (1, 0)]
    mine = lax.all_to_all(placed, "chip", split_axis=1, concat_axis=1, tiled=True)
    other = lax.ppermute(mine, "core", swap)
    hidden_own = lax.dynamic_slice_in_dim(hidden_all, first_row, tok_quarter, 0)

    def expert_rows(rows):
        flat = rows.reshape(-1, model_width)
        gate_val = jnp.dot(flat, gate_rows, preferred_element_type=jnp.float32)
        up_val = jnp.dot(flat, up_rows, preferred_element_type=jnp.float32)
        activated = (jax.nn.silu(gate_val) * up_val).astype(jnp.bfloat16)
        product = jnp.dot(activated, down_rows, preferred_element_type=jnp.float32)
        return lax.psum_scatter(
            product.astype(jnp.bfloat16).reshape(rows.shape), "exp", scatter_dimension=0, tiled=True
        )

    own_sum = expert_rows(mine)
    partner_sum = expert_rows(other)
    partner_half = lax.ppermute(partner_sum, "core", swap)
    both_halves = (own_sum.astype(jnp.float32) + partner_half.astype(jnp.float32)).astype(jnp.bfloat16)
    returned = lax.all_to_all(both_halves, "chip", split_axis=1, concat_axis=1, tiled=True)
    flattened, rank_ids = route_ranks(own_ids, experts)
    fetched = returned.reshape(capacity * experts, model_width)[rank_ids * experts + flattened]
    weighted = fetched.astype(jnp.float32) * own_gates.reshape(-1)[:, None]
    moe_out = jnp.sum(weighted.reshape(tok_quarter, -1, model_width), axis=1)
    return (hidden_own + moe_out).astype(jnp.bfloat16)


def solution(mesh):
    in_specs = (
        P(CTX, "exp"),
        P(CTX, "exp"),
        P(CTX, None),
        P(CTX, None),
        P("exp", CTX),
        P("exp", CTX),
        P("exp"),
        P("exp", None, None),
        P("exp"),
        P("exp", CTX),
        P(CTX, None),
        P(),
        P(CTX, None, "exp"),
        P(CTX, None, "exp"),
        P(CTX, "exp", None),
        P(CTX, None),
        P(CTX, None),
    )
    out_specs = P(("chip", "core", "exp"), None)
    split_mesh = Mesh(
        mesh.devices.reshape(mesh.devices.shape[0] // 2, 2, mesh.devices.shape[1]), ("chip", "core", "exp")
    )
    return jax.shard_map(local, mesh=split_mesh, in_specs=in_specs, out_specs=out_specs, check_vma=False)
```

```python
import jax
import jax.numpy as jnp
from jax import lax
from jax.sharding import Mesh, PartitionSpec as P

PAIR = 2
CTX = ("chip", "core")


eps_norm = 1e-05
top_precision = lax.Precision.HIGHEST


def combine(earlier, later):
    first_decay, first_state = earlier
    second_decay, second_state = later
    return (first_decay * second_decay, second_decay[:, None, None] * first_state + second_state)


def entering(decay, state, axis):
    place = lax.axis_index("chip") * lax.axis_size("core") + lax.axis_index("core")
    count = lax.axis_size("chip") * lax.axis_size("core")
    heads, rows, width = state.shape
    inclusive = (decay, state)
    exclusive = (jnp.ones_like(decay), jnp.zeros_like(state))
    hop = 1
    while hop < count:
        packed = jnp.concatenate(
            [inclusive[1].reshape(heads, rows * width), jnp.broadcast_to(inclusive[0][:, None], (heads, width))],
            axis=1,
        ).astype(jnp.bfloat16)
        got = lax.ppermute(packed, axis, [(i, i + hop) for i in range(count - hop)]).astype(jnp.float32)
        valid = place >= hop
        arrived = (
            jnp.where(valid, got[:, rows * width], 1.0),
            jnp.where(valid, got[:, : rows * width], 0.0).reshape(heads, rows, width),
        )
        inclusive = combine(arrived, inclusive)
        exclusive = combine(arrived, exclusive)
        hop *= 2
    return exclusive


def route_ranks(quarter_ids, experts):
    flattened = quarter_ids.reshape(-1)
    onehot = (flattened[:, None] == jnp.arange(experts, dtype=jnp.int32)[None, :]).astype(jnp.int32)
    running = jnp.cumsum(onehot, axis=0)
    rank_ids = jnp.sum(onehot * running, axis=1) - 1
    return (flattened, rank_ids)


def place_rows(normed, quarter_ids, experts, capacity):
    flattened, rank_ids = route_ranks(quarter_ids, experts)
    slot_ids = rank_ids * experts + flattened
    matches = (
        jnp.arange(capacity * experts, dtype=jnp.int32)[:, None] == slot_ids[None, :]
    ).astype(jnp.bfloat16)
    doubled = jnp.repeat(normed, quarter_ids.shape[1], axis=0)
    placed = jnp.dot(matches, doubled, preferred_element_type=jnp.float32).astype(jnp.bfloat16)
    return placed.reshape(capacity, experts, normed.shape[1])


def rms_rows(values, gain_vec):
    scaling = lax.rsqrt(jnp.mean(values * values, axis=1, keepdims=True) + eps_norm)
    return (values * scaling * gain_vec[None, :]).astype(jnp.bfloat16)


def local(
    inputs,
    gate_input,
    b_proj,
    c_proj,
    step_size,
    decay_rate,
    skip_gain,
    start_state,
    norm_gain,
    out_proj,
    residual,
    moe_gain,
    w_gate,
    w_up,
    w_down,
    route_ids,
    route_gates,
):
    tok_ctx = inputs.shape[0]
    head_count = step_size.shape[0]
    head_dim = inputs.shape[1] // head_count
    model_width = residual.shape[1]
    n_ctx = lax.axis_size("chip") * lax.axis_size("core")
    n_exp = lax.axis_size("exp")
    experts = n_ctx // PAIR
    tok_quarter = tok_ctx // n_exp
    capacity = 4 * tok_quarter // experts
    x_local = inputs.astype(jnp.float32).reshape(tok_ctx, head_count, head_dim)
    b_local = b_proj.astype(jnp.float32)
    c_local = c_proj.astype(jnp.float32)
    cumulative = jnp.cumsum(decay_rate, axis=1)
    span_total = cumulative[:, -1]
    sequence_indices = jnp.arange(tok_ctx, dtype=jnp.int32)
    causal = sequence_indices[:, None] >= sequence_indices[None, :]
    spread = jnp.where(causal[None], cumulative[:, :, None] - cumulative[:, None, :], 0.0)
    scores = jnp.dot(c_local, b_local.T, precision=top_precision)
    mixing = jnp.where(causal[None], jnp.exp(-spread), 0.0) * scores[None] * step_size[:, None, :]
    inside_part = jnp.einsum("hts,shp->thp", mixing, x_local, precision=top_precision)
    ending = jnp.exp(-(span_total[:, None] - cumulative)) * step_size
    local_state = jnp.einsum("hs,shp,sn->hpn", ending, x_local, b_local, precision=top_precision)
    prior_decay, prior_state = entering(jnp.exp(-span_total), local_state, CTX)
    incoming = prior_state + prior_decay[:, None, None] * start_state
    carried = (
        jnp.einsum("hpn,tn->thp", incoming, c_local, precision=top_precision)
        * jnp.exp(-cumulative).T[:, :, None]
    )
    ssm_out = inside_part + carried + skip_gain[None, :, None] * x_local
    gated_out = ssm_out.reshape(tok_ctx, head_count * head_dim) * jax.nn.silu(
        gate_input.astype(jnp.float32)
    )
    squares = jnp.sum(gated_out * gated_out, axis=1)
    unscaled_mix = (gated_out * norm_gain[None, :]).astype(jnp.bfloat16)
    partial_value = jnp.dot(
        unscaled_mix,
        lax.all_gather(out_proj, CTX, axis=1, tiled=True),
        preferred_element_type=jnp.float32,
    )
    width_out = partial_value.shape[1]
    summed_parts = lax.psum(
        jnp.concatenate(
            [partial_value, jnp.broadcast_to(squares[:, None], (tok_ctx, 128))], axis=1
        ).astype(jnp.bfloat16),
        "exp",
    ).astype(jnp.float32)
    scaling = lax.rsqrt(summed_parts[:, width_out] / (head_count * head_dim * n_exp) + eps_norm)
    mixed_all = summed_parts[:, :width_out] * scaling[:, None]
    gate_rows = w_gate[0]
    up_rows = w_up[0]
    down_rows = w_down[0]
    piece_width = gate_rows.shape[1]
    first_row = lax.axis_index("exp") * tok_quarter
    own_ids = lax.dynamic_slice_in_dim(route_ids, first_row, tok_quarter, 0)
    own_gates = lax.dynamic_slice_in_dim(route_gates, first_row, tok_quarter, 0)
    hidden_all = residual.astype(jnp.float32) + mixed_all
    moe_all = rms_rows(hidden_all, moe_gain)

    def place_quarter(quarter_rows, quarter_ids):
        return place_rows(quarter_rows, quarter_ids, experts, capacity)

    placed = jax.vmap(place_quarter)(
        moe_all.reshape(n_exp, tok_quarter, model_width),
        route_ids.reshape(n_exp, tok_quarter, route_ids.shape[1]),
    )
    placed = placed.reshape(n_exp * capacity, experts, model_width)
    swap = [(0, 1), (1, 0)]
    mine = lax.all_to_all(placed, "chip", split_axis=1, concat_axis=1, tiled=True)
    other = lax.ppermute(mine, "core", swap)
    hidden_own = lax.dynamic_slice_in_dim(hidden_all, first_row, tok_quarter, 0)

    def expert_rows(rows):
        flat = rows.reshape(-1, model_width)
        gate_val = jnp.dot(flat, gate_rows, preferred_element_type=jnp.float32)
        up_val = jnp.dot(flat, up_rows, preferred_element_type=jnp.float32)
        activated = (jax.nn.silu(gate_val) * up_val).astype(jnp.bfloat16)
        product = jnp.dot(activated, down_rows, preferred_element_type=jnp.float32)
        pieces = product.astype(jnp.bfloat16).reshape((n_exp, capacity) + rows.shape[1:])
        place = lax.axis_index("exp")
        total = lax.dynamic_index_in_dim(pieces, place, 0, False).astype(jnp.float32)
        for shift in range(1, n_exp):
            outgoing = lax.dynamic_index_in_dim(pieces, (place + shift) % n_exp, 0, False)
            total = total + lax.ppermute(
                outgoing, "exp", [(i, (i + shift) % n_exp) for i in range(n_exp)]
            ).astype(jnp.float32)
        return total

    own_sum = expert_rows(mine)
    partner_sum = expert_rows(other)
    partner_half = lax.ppermute(partner_sum.astype(jnp.bfloat16), "core", swap)
    both_halves = (own_sum + partner_half.astype(jnp.float32)).astype(jnp.bfloat16)
    returned = lax.all_to_all(both_halves, "chip", split_axis=1, concat_axis=1, tiled=True)
    flattened, rank_ids = route_ranks(own_ids, experts)
    fetched = returned.reshape(capacity * experts, model_width)[rank_ids * experts + flattened]
    weighted = fetched.astype(jnp.float32) * own_gates.reshape(-1)[:, None]
    moe_out = jnp.sum(weighted.reshape(tok_quarter, -1, model_width), axis=1)
    return (hidden_own + moe_out).astype(jnp.bfloat16)


def solution(mesh):
    in_specs = (
        P(CTX, "exp"),
        P(CTX, "exp"),
        P(CTX, None),
        P(CTX, None),
        P("exp", CTX),
        P("exp", CTX),
        P("exp"),
        P("exp", None, None),
        P("exp"),
        P("exp", CTX),
        P(CTX, None),
        P(),
        P(CTX, None, "exp"),
        P(CTX, None, "exp"),
        P(CTX, "exp", None),
        P(CTX, None),
        P(CTX, None),
    )
    out_specs = P(("chip", "core", "exp"), None)
    split_mesh = Mesh(
        mesh.devices.reshape(mesh.devices.shape[0] // 2, 2, mesh.devices.shape[1]), ("chip", "core", "exp")
    )
    return jax.shard_map(local, mesh=split_mesh, in_specs=in_specs, out_specs=out_specs, check_vma=False)
```

```python
import jax
import jax.numpy as jnp
from jax import lax
from jax.sharding import Mesh, PartitionSpec as P

PAIR = 2
CTX = ("chip", "core")


eps_norm = 1e-05
top_precision = lax.Precision.HIGHEST


def combine(earlier, later):
    first_decay, first_state = earlier
    second_decay, second_state = later
    return (first_decay * second_decay, second_decay[:, None, None] * first_state + second_state)


def entering(decay, state, axis):
    place = lax.axis_index("chip") * lax.axis_size("core") + lax.axis_index("core")
    count = lax.axis_size("chip") * lax.axis_size("core")
    heads, rows, width = state.shape
    inclusive = (decay, state)
    exclusive = (jnp.ones_like(decay), jnp.zeros_like(state))
    hop = 1
    while hop < count:
        packed = jnp.concatenate(
            [inclusive[1].reshape(heads, rows * width), jnp.broadcast_to(inclusive[0][:, None], (heads, width))],
            axis=1,
        ).astype(jnp.bfloat16)
        got = lax.ppermute(packed, axis, [(i, i + hop) for i in range(count - hop)]).astype(jnp.float32)
        valid = place >= hop
        arrived = (
            jnp.where(valid, got[:, rows * width], 1.0),
            jnp.where(valid, got[:, : rows * width], 0.0).reshape(heads, rows, width),
        )
        inclusive = combine(arrived, inclusive)
        exclusive = combine(arrived, exclusive)
        hop *= 2
    return exclusive


def route_ranks(quarter_ids, experts):
    flattened = quarter_ids.reshape(-1)
    onehot = (flattened[:, None] == jnp.arange(experts, dtype=jnp.int32)[None, :]).astype(jnp.int32)
    running = jnp.cumsum(onehot, axis=0)
    rank_ids = jnp.sum(onehot * running, axis=1) - 1
    return (flattened, rank_ids)


def place_rows(normed, quarter_ids, experts, capacity):
    flattened, rank_ids = route_ranks(quarter_ids, experts)
    slot_ids = rank_ids * experts + flattened
    matches = (
        jnp.arange(capacity * experts, dtype=jnp.int32)[:, None] == slot_ids[None, :]
    ).astype(jnp.bfloat16)
    doubled = jnp.repeat(normed, quarter_ids.shape[1], axis=0)
    placed = jnp.dot(matches, doubled, preferred_element_type=jnp.float32).astype(jnp.bfloat16)
    return placed.reshape(capacity, experts, normed.shape[1])


def rms_rows(values, gain_vec):
    scaling = lax.rsqrt(jnp.mean(values * values, axis=1, keepdims=True) + eps_norm)
    return (values * scaling * gain_vec[None, :]).astype(jnp.bfloat16)


def local(
    inputs,
    gate_input,
    b_proj,
    c_proj,
    step_size,
    decay_rate,
    skip_gain,
    start_state,
    norm_gain,
    out_proj,
    residual,
    moe_gain,
    w_gate,
    w_up,
    w_down,
    route_ids,
    route_gates,
):
    tok_ctx = inputs.shape[0]
    head_count = step_size.shape[0]
    head_dim = inputs.shape[1] // head_count
    model_width = residual.shape[1]
    n_ctx = lax.axis_size("chip") * lax.axis_size("core")
    n_exp = lax.axis_size("exp")
    experts = n_ctx // PAIR
    tok_quarter = tok_ctx // n_exp
    capacity = 4 * tok_quarter // experts
    x_local = inputs.astype(jnp.float32).reshape(tok_ctx, head_count, head_dim)
    b_local = b_proj.astype(jnp.float32)
    c_local = c_proj.astype(jnp.float32)
    cumulative = jnp.cumsum(decay_rate, axis=1)
    span_total = cumulative[:, -1]
    sequence_indices = jnp.arange(tok_ctx, dtype=jnp.int32)
    causal = sequence_indices[:, None] >= sequence_indices[None, :]
    spread = jnp.where(causal[None], cumulative[:, :, None] - cumulative[:, None, :], 0.0)
    scores = jnp.dot(c_local, b_local.T, precision=top_precision)
    mixing = jnp.where(causal[None], jnp.exp(-spread), 0.0) * scores[None] * step_size[:, None, :]
    inside_part = jnp.einsum("hts,shp->thp", mixing, x_local, precision=top_precision)
    ending = jnp.exp(-(span_total[:, None] - cumulative)) * step_size
    local_state = jnp.einsum("hs,shp,sn->hpn", ending, x_local, b_local, precision=top_precision)
    prior_decay, prior_state = entering(jnp.exp(-span_total), local_state, CTX)
    incoming = prior_state + prior_decay[:, None, None] * start_state
    carried = (
        jnp.einsum("hpn,tn->thp", incoming, c_local, precision=top_precision)
        * jnp.exp(-cumulative).T[:, :, None]
    )
    ssm_out = inside_part + carried + skip_gain[None, :, None] * x_local
    gated_out = ssm_out.reshape(tok_ctx, head_count * head_dim) * jax.nn.silu(
        gate_input.astype(jnp.float32)
    )
    squares = jnp.sum(gated_out * gated_out, axis=1)
    unscaled_mix = (gated_out * norm_gain[None, :]).astype(jnp.bfloat16)
    partial_value = jnp.dot(
        unscaled_mix,
        lax.all_gather(out_proj, CTX, axis=1, tiled=True),
        preferred_element_type=jnp.float32,
    )
    width_out = partial_value.shape[1]
    summed_parts = lax.psum(
        jnp.concatenate(
            [partial_value, jnp.broadcast_to(squares[:, None], (tok_ctx, 128))], axis=1
        ).astype(jnp.bfloat16),
        "exp",
    ).astype(jnp.float32)
    scaling = lax.rsqrt(summed_parts[:, width_out] / (head_count * head_dim * n_exp) + eps_norm)
    mixed_all = summed_parts[:, :width_out] * scaling[:, None]
    gate_rows = w_gate[0]
    up_rows = w_up[0]
    down_rows = w_down[0]
    piece_width = gate_rows.shape[1]
    first_row = lax.axis_index("exp") * tok_quarter
    own_ids = lax.dynamic_slice_in_dim(route_ids, first_row, tok_quarter, 0)
    own_gates = lax.dynamic_slice_in_dim(route_gates, first_row, tok_quarter, 0)
    hidden_all = residual.astype(jnp.float32) + mixed_all
    moe_all = rms_rows(hidden_all, moe_gain)

    def place_quarter(quarter_rows, quarter_ids):
        return place_rows(quarter_rows, quarter_ids, experts, capacity)

    placed = jax.vmap(place_quarter)(
        moe_all.reshape(n_exp, tok_quarter, model_width),
        route_ids.reshape(n_exp, tok_quarter, route_ids.shape[1]),
    )
    placed = placed.reshape(n_exp * capacity, experts, model_width)
    swap = [(0, 1), (1, 0)]
    hidden_own = lax.dynamic_slice_in_dim(hidden_all, first_row, tok_quarter, 0)

    def expert_rows(rows):
        flat = rows.reshape(-1, model_width)
        gate_val = jnp.dot(flat, gate_rows, preferred_element_type=jnp.float32)
        up_val = jnp.dot(flat, up_rows, preferred_element_type=jnp.float32)
        activated = (jax.nn.silu(gate_val) * up_val).astype(jnp.bfloat16)
        product = jnp.dot(activated, down_rows, preferred_element_type=jnp.float32)
        pieces = product.astype(jnp.bfloat16).reshape((n_exp, rows.shape[0] // n_exp) + rows.shape[1:])
        place = lax.axis_index("exp")
        total = lax.dynamic_index_in_dim(pieces, place, 0, False).astype(jnp.float32)
        for shift in range(1, n_exp):
            outgoing = lax.dynamic_index_in_dim(pieces, (place + shift) % n_exp, 0, False)
            total = total + lax.ppermute(
                outgoing, "exp", [(i, (i + shift) % n_exp) for i in range(n_exp)]
            ).astype(jnp.float32)
        return total

    swap = [(0, 1), (1, 0)]
    by_quarter = placed.reshape(n_exp, capacity, experts, model_width)
    rank_parts = 2
    part_rows = capacity // rank_parts
    finished = []
    for part in range(rank_parts):
        chunk = by_quarter[:, part * part_rows : (part + 1) * part_rows].reshape(
            n_exp * part_rows, experts, model_width
        )
        mine = lax.all_to_all(chunk, "chip", split_axis=1, concat_axis=1, tiled=True)
        other = lax.ppermute(mine, "core", swap)
        own_sum = expert_rows(mine)
        partner_sum = expert_rows(other)
        partner_half = lax.ppermute(partner_sum.astype(jnp.bfloat16), "core", swap)
        finished.append((own_sum + partner_half.astype(jnp.float32)).astype(jnp.bfloat16))
    both_halves = jnp.concatenate(finished, axis=0)
    returned = lax.all_to_all(both_halves, "chip", split_axis=1, concat_axis=1, tiled=True)
    flattened, rank_ids = route_ranks(own_ids, experts)
    fetched = returned.reshape(capacity * experts, model_width)[rank_ids * experts + flattened]
    weighted = fetched.astype(jnp.float32) * own_gates.reshape(-1)[:, None]
    moe_out = jnp.sum(weighted.reshape(tok_quarter, -1, model_width), axis=1)
    return (hidden_own + moe_out).astype(jnp.bfloat16)


def solution(mesh):
    in_specs = (
        P(CTX, "exp"),
        P(CTX, "exp"),
        P(CTX, None),
        P(CTX, None),
        P("exp", CTX),
        P("exp", CTX),
        P("exp"),
        P("exp", None, None),
        P("exp"),
        P("exp", CTX),
        P(CTX, None),
        P(),
        P(CTX, None, "exp"),
        P(CTX, None, "exp"),
        P(CTX, "exp", None),
        P(CTX, None),
        P(CTX, None),
    )
    out_specs = P(("chip", "core", "exp"), None)
    split_mesh = Mesh(
        mesh.devices.reshape(mesh.devices.shape[0] // 2, 2, mesh.devices.shape[1]), ("chip", "core", "exp")
    )
    return jax.shard_map(local, mesh=split_mesh, in_specs=in_specs, out_specs=out_specs, check_vma=False)
```

```python
import functools

import jax
import jax.numpy as jnp
from jax import lax
from jax.experimental import pallas as pl
from jax.experimental.pallas import tpu as pltpu
from jax.sharding import Mesh, PartitionSpec as P

PAIR = 2
CTX = ("chip", "core")


eps_norm = 1e-05
top_precision = lax.Precision.HIGHEST


def scan_kernel(count, decay_ref, state_ref, out_decay, out_state, inc_buf, recv_buf,
                inc_decay, inc_state, send_sem, recv_sem):
    chip = lax.axis_index("chip")
    core = lax.axis_index("core")
    member = lax.axis_index("exp")
    place = chip * 2 + core
    width = state_ref.shape[1]
    hops = []
    hop = 1
    while hop < count:
        hops.append(hop)
        hop *= 2

    def target(index):
        return (index // 2, index % 2, member)

    barrier = pltpu.get_barrier_semaphore()
    partners = 0
    for hop in hops:
        ahead = place + hop < count
        behind = place >= hop
        partners = partners + ahead.astype(jnp.int32) + behind.astype(jnp.int32)

        @pl.when(ahead)
        def _():
            pl.semaphore_signal(barrier, inc=1, device_id=target(place + hop), device_id_type=pl.DeviceIdType.MESH)

        @pl.when(behind)
        def _():
            pl.semaphore_signal(barrier, inc=1, device_id=target(place - hop), device_id_type=pl.DeviceIdType.MESH)

    pl.semaphore_wait(barrier, partners)
    inc_decay[...] = decay_ref[...]
    inc_state[...] = state_ref[...]
    out_decay[...] = jnp.ones_like(out_decay)
    out_state[...] = jnp.zeros_like(out_state)
    for step, hop in enumerate(hops):
        ahead = place + hop < count
        behind = place >= hop
        inc_buf[step, :, :width] = inc_state[...].astype(jnp.bfloat16)
        inc_buf[step, :, width:] = inc_decay[...].astype(jnp.bfloat16)
        copy = pltpu.make_async_remote_copy(
            src_ref=inc_buf.at[step],
            dst_ref=recv_buf.at[step],
            send_sem=send_sem.at[step],
            recv_sem=recv_sem.at[step],
            device_id=target(jnp.minimum(place + hop, count - 1)),
            device_id_type=pl.DeviceIdType.MESH,
        )

        @pl.when(ahead)
        def _():
            copy.start()

        @pl.when(behind)
        def _():
            copy.wait_recv()
            got_state = recv_buf[step, :, :width].astype(jnp.float32)
            got_decay = recv_buf[step, :, width:].astype(jnp.float32)
            inc_state[...] = inc_decay[:, 0:1] * got_state + inc_state[...]
            inc_decay[...] = got_decay * inc_decay[...]
            out_state[...] = out_decay[:, 0:1] * got_state + out_state[...]
            out_decay[...] = got_decay * out_decay[...]

        @pl.when(ahead)
        def _():
            copy.wait_send()


def entering(decay, state, count):
    heads, rows, width = state.shape
    flat = rows * width
    lanes = 128
    vmem = pl.BlockSpec(memory_space=pltpu.VMEM)
    steps = max(1, (count - 1).bit_length())
    out_decay, out_state = pl.pallas_call(
        functools.partial(scan_kernel, count),
        out_shape=(
            jax.ShapeDtypeStruct((heads, lanes), jnp.float32),
            jax.ShapeDtypeStruct((heads, flat), jnp.float32),
        ),
        in_specs=[vmem, vmem],
        out_specs=(vmem, vmem),
        scratch_shapes=[
            pltpu.VMEM((steps, heads, flat + lanes), jnp.bfloat16),
            pltpu.VMEM((steps, heads, flat + lanes), jnp.bfloat16),
            pltpu.VMEM((heads, lanes), jnp.float32),
            pltpu.VMEM((heads, flat), jnp.float32),
            pltpu.SemaphoreType.DMA((steps,)),
            pltpu.SemaphoreType.DMA((steps,)),
        ],
        compiler_params=pltpu.CompilerParams(collective_id=0, has_side_effects=True),
    )(jnp.broadcast_to(decay[:, None], (heads, lanes)), state.reshape(heads, flat))
    return out_decay[:, 0], out_state.reshape(heads, rows, width)


def route_ranks(quarter_ids, experts):
    flattened = quarter_ids.reshape(-1)
    onehot = (flattened[:, None] == jnp.arange(experts, dtype=jnp.int32)[None, :]).astype(jnp.int32)
    running = jnp.cumsum(onehot, axis=0)
    rank_ids = jnp.sum(onehot * running, axis=1) - 1
    return (flattened, rank_ids)


def place_rows(normed, quarter_ids, experts, capacity):
    flattened, rank_ids = route_ranks(quarter_ids, experts)
    slot_ids = rank_ids * experts + flattened
    matches = (
        jnp.arange(capacity * experts, dtype=jnp.int32)[:, None] == slot_ids[None, :]
    ).astype(jnp.bfloat16)
    doubled = jnp.repeat(normed, quarter_ids.shape[1], axis=0)
    placed = jnp.dot(matches, doubled, preferred_element_type=jnp.float32).astype(jnp.bfloat16)
    return placed.reshape(capacity, experts, normed.shape[1])


def rms_rows(values, gain_vec):
    scaling = lax.rsqrt(jnp.mean(values * values, axis=1, keepdims=True) + eps_norm)
    return (values * scaling * gain_vec[None, :]).astype(jnp.bfloat16)


def local(
    inputs,
    gate_input,
    b_proj,
    c_proj,
    step_size,
    decay_rate,
    skip_gain,
    start_state,
    norm_gain,
    out_proj,
    residual,
    moe_gain,
    w_gate,
    w_up,
    w_down,
    route_ids,
    route_gates,
):
    tok_ctx = inputs.shape[0]
    head_count = step_size.shape[0]
    head_dim = inputs.shape[1] // head_count
    model_width = residual.shape[1]
    n_ctx = lax.axis_size("chip") * lax.axis_size("core")
    n_exp = lax.axis_size("exp")
    experts = n_ctx // PAIR
    tok_quarter = tok_ctx // n_exp
    capacity = 4 * tok_quarter // experts
    x_local = inputs.astype(jnp.float32).reshape(tok_ctx, head_count, head_dim)
    b_local = b_proj.astype(jnp.float32)
    c_local = c_proj.astype(jnp.float32)
    cumulative = jnp.cumsum(decay_rate, axis=1)
    span_total = cumulative[:, -1]
    sequence_indices = jnp.arange(tok_ctx, dtype=jnp.int32)
    causal = sequence_indices[:, None] >= sequence_indices[None, :]
    spread = jnp.where(causal[None], cumulative[:, :, None] - cumulative[:, None, :], 0.0)
    scores = jnp.dot(c_local, b_local.T, precision=top_precision)
    mixing = jnp.where(causal[None], jnp.exp(-spread), 0.0) * scores[None] * step_size[:, None, :]
    inside_part = jnp.einsum("hts,shp->thp", mixing, x_local, precision=top_precision)
    ending = jnp.exp(-(span_total[:, None] - cumulative)) * step_size
    local_state = jnp.einsum("hs,shp,sn->hpn", ending, x_local, b_local, precision=top_precision)
    prior_decay, prior_state = entering(jnp.exp(-span_total), local_state, n_ctx)
    incoming = prior_state + prior_decay[:, None, None] * start_state
    carried = (
        jnp.einsum("hpn,tn->thp", incoming, c_local, precision=top_precision)
        * jnp.exp(-cumulative).T[:, :, None]
    )
    ssm_out = inside_part + carried + skip_gain[None, :, None] * x_local
    gated_out = ssm_out.reshape(tok_ctx, head_count * head_dim) * jax.nn.silu(
        gate_input.astype(jnp.float32)
    )
    squares = jnp.sum(gated_out * gated_out, axis=1)
    unscaled_mix = (gated_out * norm_gain[None, :]).astype(jnp.bfloat16)
    partial_value = jnp.dot(
        unscaled_mix,
        lax.all_gather(out_proj, CTX, axis=1, tiled=True),
        preferred_element_type=jnp.float32,
    )
    width_out = partial_value.shape[1]
    summed_parts = lax.psum(
        jnp.concatenate(
            [partial_value, jnp.broadcast_to(squares[:, None], (tok_ctx, 128))], axis=1
        ).astype(jnp.bfloat16),
        "exp",
    ).astype(jnp.float32)
    scaling = lax.rsqrt(summed_parts[:, width_out] / (head_count * head_dim * n_exp) + eps_norm)
    mixed_all = summed_parts[:, :width_out] * scaling[:, None]
    gate_rows = w_gate[0]
    up_rows = w_up[0]
    down_rows = w_down[0]
    piece_width = gate_rows.shape[1]
    first_row = lax.axis_index("exp") * tok_quarter
    own_ids = lax.dynamic_slice_in_dim(route_ids, first_row, tok_quarter, 0)
    own_gates = lax.dynamic_slice_in_dim(route_gates, first_row, tok_quarter, 0)
    hidden_all = residual.astype(jnp.float32) + mixed_all
    moe_all = rms_rows(hidden_all, moe_gain)

    def place_quarter(quarter_rows, quarter_ids):
        return place_rows(quarter_rows, quarter_ids, experts, capacity)

    placed = jax.vmap(place_quarter)(
        moe_all.reshape(n_exp, tok_quarter, model_width),
        route_ids.reshape(n_exp, tok_quarter, route_ids.shape[1]),
    )
    placed = placed.reshape(n_exp * capacity, experts, model_width)
    swap = [(0, 1), (1, 0)]
    mine = lax.all_to_all(placed, "chip", split_axis=1, concat_axis=1, tiled=True)
    other = lax.ppermute(mine, "core", swap)
    hidden_own = lax.dynamic_slice_in_dim(hidden_all, first_row, tok_quarter, 0)

    def expert_rows(rows):
        flat = rows.reshape(-1, model_width)
        gate_val = jnp.dot(flat, gate_rows, preferred_element_type=jnp.float32)
        up_val = jnp.dot(flat, up_rows, preferred_element_type=jnp.float32)
        activated = (jax.nn.silu(gate_val) * up_val).astype(jnp.bfloat16)
        product = jnp.dot(activated, down_rows, preferred_element_type=jnp.float32)
        return lax.psum_scatter(
            product.astype(jnp.bfloat16).reshape(rows.shape), "exp", scatter_dimension=0, tiled=True
        )

    own_sum = expert_rows(mine)
    partner_sum = expert_rows(other)
    partner_half = lax.ppermute(partner_sum, "core", swap)
    both_halves = (own_sum.astype(jnp.float32) + partner_half.astype(jnp.float32)).astype(jnp.bfloat16)
    returned = lax.all_to_all(both_halves, "chip", split_axis=1, concat_axis=1, tiled=True)
    flattened, rank_ids = route_ranks(own_ids, experts)
    fetched = returned.reshape(capacity * experts, model_width)[rank_ids * experts + flattened]
    weighted = fetched.astype(jnp.float32) * own_gates.reshape(-1)[:, None]
    moe_out = jnp.sum(weighted.reshape(tok_quarter, -1, model_width), axis=1)
    return (hidden_own + moe_out).astype(jnp.bfloat16)


def solution(mesh):
    in_specs = (
        P(CTX, "exp"),
        P(CTX, "exp"),
        P(CTX, None),
        P(CTX, None),
        P("exp", CTX),
        P("exp", CTX),
        P("exp"),
        P("exp", None, None),
        P("exp"),
        P("exp", CTX),
        P(CTX, None),
        P(),
        P(CTX, None, "exp"),
        P(CTX, None, "exp"),
        P(CTX, "exp", None),
        P(CTX, None),
        P(CTX, None),
    )
    out_specs = P(("chip", "core", "exp"), None)
    split_mesh = Mesh(
        mesh.devices.reshape(mesh.devices.shape[0] // 2, 2, mesh.devices.shape[1]), ("chip", "core", "exp")
    )
    return jax.shard_map(local, mesh=split_mesh, in_specs=in_specs, out_specs=out_specs, check_vma=False)
```

```python
import functools

import jax
import jax.numpy as jnp
from jax import lax
from jax.experimental import pallas as pl
from jax.experimental.pallas import tpu as pltpu
from jax.sharding import Mesh, PartitionSpec as P

PAIR = 2
CTX = ("chip", "core")


eps_norm = 1e-05
top_precision = lax.Precision.HIGHEST


def scan_kernel(count, decay_ref, state_ref, out_decay, out_state, inc_buf, recv_buf,
                inc_decay, inc_state, send_sem, recv_sem):
    chip = lax.axis_index("chip")
    core = lax.axis_index("core")
    member = lax.axis_index("exp")
    place = chip * 2 + core
    width = state_ref.shape[1]
    hops = []
    hop = 1
    while hop < count:
        hops.append(hop)
        hop *= 2

    def target(index):
        return (index // 2, index % 2, member)

    barrier = pltpu.get_barrier_semaphore()
    partners = 0
    for hop in hops:
        ahead = place + hop < count
        behind = place >= hop
        partners = partners + ahead.astype(jnp.int32) + behind.astype(jnp.int32)

        @pl.when(ahead)
        def _():
            pl.semaphore_signal(barrier, inc=1, device_id=target(place + hop), device_id_type=pl.DeviceIdType.MESH)

        @pl.when(behind)
        def _():
            pl.semaphore_signal(barrier, inc=1, device_id=target(place - hop), device_id_type=pl.DeviceIdType.MESH)

    pl.semaphore_wait(barrier, partners)
    inc_decay[...] = decay_ref[...]
    inc_state[...] = state_ref[...]
    out_decay[...] = jnp.ones_like(out_decay)
    out_state[...] = jnp.zeros_like(out_state)
    for step, hop in enumerate(hops):
        ahead = place + hop < count
        behind = place >= hop
        inc_buf[step, :, :width] = inc_state[...].astype(jnp.bfloat16)
        inc_buf[step, :, width:] = inc_decay[...].astype(jnp.bfloat16)
        copy = pltpu.make_async_remote_copy(
            src_ref=inc_buf.at[step],
            dst_ref=recv_buf.at[step],
            send_sem=send_sem.at[step],
            recv_sem=recv_sem.at[step],
            device_id=target(jnp.minimum(place + hop, count - 1)),
            device_id_type=pl.DeviceIdType.MESH,
        )

        @pl.when(ahead)
        def _():
            copy.start()

        @pl.when(behind)
        def _():
            copy.wait_recv()
            got_state = recv_buf[step, :, :width].astype(jnp.float32)
            got_decay = recv_buf[step, :, width:].astype(jnp.float32)
            inc_state[...] = inc_decay[:, 0:1] * got_state + inc_state[...]
            inc_decay[...] = got_decay * inc_decay[...]
            out_state[...] = out_decay[:, 0:1] * got_state + out_state[...]
            out_decay[...] = got_decay * out_decay[...]

        @pl.when(ahead)
        def _():
            copy.wait_send()


def entering(decay, state, count):
    heads, rows, width = state.shape
    flat = rows * width
    lanes = 128
    vmem = pl.BlockSpec(memory_space=pltpu.VMEM)
    steps = max(1, (count - 1).bit_length())
    out_decay, out_state = pl.pallas_call(
        functools.partial(scan_kernel, count),
        out_shape=(
            jax.ShapeDtypeStruct((heads, lanes), jnp.float32),
            jax.ShapeDtypeStruct((heads, flat), jnp.float32),
        ),
        in_specs=[vmem, vmem],
        out_specs=(vmem, vmem),
        scratch_shapes=[
            pltpu.VMEM((steps, heads, flat + lanes), jnp.bfloat16),
            pltpu.VMEM((steps, heads, flat + lanes), jnp.bfloat16),
            pltpu.VMEM((heads, lanes), jnp.float32),
            pltpu.VMEM((heads, flat), jnp.float32),
            pltpu.SemaphoreType.DMA((steps,)),
            pltpu.SemaphoreType.DMA((steps,)),
        ],
        compiler_params=pltpu.CompilerParams(collective_id=0, has_side_effects=True),
    )(jnp.broadcast_to(decay[:, None], (heads, lanes)), state.reshape(heads, flat))
    return out_decay[:, 0], out_state.reshape(heads, rows, width)


def route_ranks(quarter_ids, experts):
    flattened = quarter_ids.reshape(-1)
    onehot = (flattened[:, None] == jnp.arange(experts, dtype=jnp.int32)[None, :]).astype(jnp.int32)
    running = jnp.cumsum(onehot, axis=0)
    rank_ids = jnp.sum(onehot * running, axis=1) - 1
    return (flattened, rank_ids)


def place_rows(normed, quarter_ids, experts, capacity):
    flattened, rank_ids = route_ranks(quarter_ids, experts)
    slot_ids = rank_ids * experts + flattened
    matches = (
        jnp.arange(capacity * experts, dtype=jnp.int32)[:, None] == slot_ids[None, :]
    ).astype(jnp.bfloat16)
    doubled = jnp.repeat(normed, quarter_ids.shape[1], axis=0)
    placed = jnp.dot(matches, doubled, preferred_element_type=jnp.float32).astype(jnp.bfloat16)
    return placed.reshape(capacity, experts, normed.shape[1])


def rms_rows(values, gain_vec):
    scaling = lax.rsqrt(jnp.mean(values * values, axis=1, keepdims=True) + eps_norm)
    return (values * scaling * gain_vec[None, :]).astype(jnp.bfloat16)


def local(
    inputs,
    gate_input,
    b_proj,
    c_proj,
    step_size,
    decay_rate,
    skip_gain,
    start_state,
    norm_gain,
    out_proj,
    residual,
    moe_gain,
    w_gate,
    w_up,
    w_down,
    route_ids,
    route_gates,
):
    tok_ctx = inputs.shape[0]
    head_count = step_size.shape[0]
    head_dim = inputs.shape[1] // head_count
    model_width = residual.shape[1]
    n_ctx = lax.axis_size("chip") * lax.axis_size("core")
    n_exp = lax.axis_size("exp")
    experts = n_ctx // PAIR
    tok_quarter = tok_ctx // n_exp
    capacity = 4 * tok_quarter // experts
    x_local = inputs.astype(jnp.float32).reshape(tok_ctx, head_count, head_dim)
    b_local = b_proj.astype(jnp.float32)
    c_local = c_proj.astype(jnp.float32)
    cumulative = jnp.cumsum(decay_rate, axis=1)
    span_total = cumulative[:, -1]
    sequence_indices = jnp.arange(tok_ctx, dtype=jnp.int32)
    causal = sequence_indices[:, None] >= sequence_indices[None, :]
    spread = jnp.where(causal[None], cumulative[:, :, None] - cumulative[:, None, :], 0.0)
    scores = jnp.dot(c_local, b_local.T, precision=top_precision)
    mixing = jnp.where(causal[None], jnp.exp(-spread), 0.0) * scores[None] * step_size[:, None, :]
    inside_part = jnp.einsum("hts,shp->thp", mixing, x_local, precision=top_precision)
    ending = jnp.exp(-(span_total[:, None] - cumulative)) * step_size
    local_state = jnp.einsum("hs,shp,sn->hpn", ending, x_local, b_local, precision=top_precision)
    prior_decay, prior_state = entering(jnp.exp(-span_total), local_state, n_ctx)
    incoming = prior_state + prior_decay[:, None, None] * start_state
    carried = (
        jnp.einsum("hpn,tn->thp", incoming, c_local, precision=top_precision)
        * jnp.exp(-cumulative).T[:, :, None]
    )
    ssm_out = inside_part + carried + skip_gain[None, :, None] * x_local
    gated_out = ssm_out.reshape(tok_ctx, head_count * head_dim) * jax.nn.silu(
        gate_input.astype(jnp.float32)
    )
    squares = jnp.sum(gated_out * gated_out, axis=1)
    unscaled_mix = (gated_out * norm_gain[None, :]).astype(jnp.bfloat16)
    partial_value = jnp.dot(
        unscaled_mix,
        lax.all_gather(out_proj, CTX, axis=1, tiled=True),
        preferred_element_type=jnp.float32,
    )
    width_out = partial_value.shape[1]
    joined = jnp.concatenate(
        [partial_value, jnp.broadcast_to(squares[:, None], (tok_ctx, 128))], axis=1
    ).astype(jnp.bfloat16)
    quarters = lax.all_to_all(
        joined.reshape(n_exp, tok_quarter, joined.shape[1]), "exp", split_axis=0, concat_axis=0, tiled=True
    )
    quarter_sum = jnp.sum(quarters.astype(jnp.float32), axis=0).astype(jnp.bfloat16)
    summed_parts = lax.all_to_all(
        jnp.broadcast_to(quarter_sum[None], (n_exp,) + quarter_sum.shape), "exp", split_axis=0, concat_axis=0, tiled=True
    ).reshape(tok_ctx, joined.shape[1]).astype(jnp.float32)
    scaling = lax.rsqrt(summed_parts[:, width_out] / (head_count * head_dim * n_exp) + eps_norm)
    mixed_all = summed_parts[:, :width_out] * scaling[:, None]
    gate_rows = w_gate[0]
    up_rows = w_up[0]
    down_rows = w_down[0]
    piece_width = gate_rows.shape[1]
    first_row = lax.axis_index("exp") * tok_quarter
    own_ids = lax.dynamic_slice_in_dim(route_ids, first_row, tok_quarter, 0)
    own_gates = lax.dynamic_slice_in_dim(route_gates, first_row, tok_quarter, 0)
    hidden_all = residual.astype(jnp.float32) + mixed_all
    moe_all = rms_rows(hidden_all, moe_gain)

    def place_quarter(quarter_rows, quarter_ids):
        return place_rows(quarter_rows, quarter_ids, experts, capacity)

    placed = jax.vmap(place_quarter)(
        moe_all.reshape(n_exp, tok_quarter, model_width),
        route_ids.reshape(n_exp, tok_quarter, route_ids.shape[1]),
    )
    placed = placed.reshape(n_exp * capacity, experts, model_width)
    swap = [(0, 1), (1, 0)]
    mine = lax.all_to_all(placed, "chip", split_axis=1, concat_axis=1, tiled=True)
    other = lax.ppermute(mine, "core", swap)
    hidden_own = lax.dynamic_slice_in_dim(hidden_all, first_row, tok_quarter, 0)

    def expert_rows(rows):
        flat = rows.reshape(-1, model_width)
        gate_val = jnp.dot(flat, gate_rows, preferred_element_type=jnp.float32)
        up_val = jnp.dot(flat, up_rows, preferred_element_type=jnp.float32)
        activated = (jax.nn.silu(gate_val) * up_val).astype(jnp.bfloat16)
        product = jnp.dot(activated, down_rows, preferred_element_type=jnp.float32)
        return lax.psum_scatter(
            product.astype(jnp.bfloat16).reshape(rows.shape), "exp", scatter_dimension=0, tiled=True
        )

    own_sum = expert_rows(mine)
    partner_sum = expert_rows(other)
    partner_half = lax.ppermute(partner_sum, "core", swap)
    both_halves = (own_sum.astype(jnp.float32) + partner_half.astype(jnp.float32)).astype(jnp.bfloat16)
    returned = lax.all_to_all(both_halves, "chip", split_axis=1, concat_axis=1, tiled=True)
    flattened, rank_ids = route_ranks(own_ids, experts)
    fetched = returned.reshape(capacity * experts, model_width)[rank_ids * experts + flattened]
    weighted = fetched.astype(jnp.float32) * own_gates.reshape(-1)[:, None]
    moe_out = jnp.sum(weighted.reshape(tok_quarter, -1, model_width), axis=1)
    return (hidden_own + moe_out).astype(jnp.bfloat16)


def solution(mesh):
    in_specs = (
        P(CTX, "exp"),
        P(CTX, "exp"),
        P(CTX, None),
        P(CTX, None),
        P("exp", CTX),
        P("exp", CTX),
        P("exp"),
        P("exp", None, None),
        P("exp"),
        P("exp", CTX),
        P(CTX, None),
        P(),
        P(CTX, None, "exp"),
        P(CTX, None, "exp"),
        P(CTX, "exp", None),
        P(CTX, None),
        P(CTX, None),
    )
    out_specs = P(("chip", "core", "exp"), None)
    split_mesh = Mesh(
        mesh.devices.reshape(mesh.devices.shape[0] // 2, 2, mesh.devices.shape[1]), ("chip", "core", "exp")
    )
    return jax.shard_map(local, mesh=split_mesh, in_specs=in_specs, out_specs=out_specs, check_vma=False)
```

```python
import functools

import jax
import jax.numpy as jnp
from jax import lax
from jax.experimental import pallas as pl
from jax.experimental.pallas import tpu as pltpu
from jax.sharding import Mesh, PartitionSpec as P

PAIR = 2
CTX = ("chip", "core")


eps_norm = 1e-05
top_precision = lax.Precision.HIGHEST


def scan_kernel(count, decay_ref, state_ref, out_decay, out_state, inc_buf, recv_buf,
                inc_decay, inc_state, send_sem, recv_sem):
    chip = lax.axis_index("chip")
    core = lax.axis_index("core")
    member = lax.axis_index("exp")
    place = chip * 2 + core
    width = state_ref.shape[1]
    hops = []
    hop = 1
    while hop < count:
        hops.append(hop)
        hop *= 2

    def target(index):
        return (index // 2, index % 2, member)

    barrier = pltpu.get_barrier_semaphore()
    partners = 0
    for hop in hops:
        ahead = place + hop < count
        behind = place >= hop
        partners = partners + ahead.astype(jnp.int32) + behind.astype(jnp.int32)

        @pl.when(ahead)
        def _():
            pl.semaphore_signal(barrier, inc=1, device_id=target(place + hop), device_id_type=pl.DeviceIdType.MESH)

        @pl.when(behind)
        def _():
            pl.semaphore_signal(barrier, inc=1, device_id=target(place - hop), device_id_type=pl.DeviceIdType.MESH)

    pl.semaphore_wait(barrier, partners)
    inc_decay[...] = decay_ref[...]
    inc_state[...] = state_ref[...]
    out_decay[...] = jnp.ones_like(out_decay)
    out_state[...] = jnp.zeros_like(out_state)
    for step, hop in enumerate(hops):
        ahead = place + hop < count
        behind = place >= hop
        inc_buf[step, :, :width] = inc_state[...].astype(jnp.bfloat16)
        inc_buf[step, :, width:] = inc_decay[...].astype(jnp.bfloat16)
        copy = pltpu.make_async_remote_copy(
            src_ref=inc_buf.at[step],
            dst_ref=recv_buf.at[step],
            send_sem=send_sem.at[step],
            recv_sem=recv_sem.at[step],
            device_id=target(jnp.minimum(place + hop, count - 1)),
            device_id_type=pl.DeviceIdType.MESH,
        )

        @pl.when(ahead)
        def _():
            copy.start()

        @pl.when(behind)
        def _():
            copy.wait_recv()
            got_state = recv_buf[step, :, :width].astype(jnp.float32)
            got_decay = recv_buf[step, :, width:].astype(jnp.float32)
            inc_state[...] = inc_decay[:, 0:1] * got_state + inc_state[...]
            inc_decay[...] = got_decay * inc_decay[...]
            out_state[...] = out_decay[:, 0:1] * got_state + out_state[...]
            out_decay[...] = got_decay * out_decay[...]

        @pl.when(ahead)
        def _():
            copy.wait_send()


def entering(decay, state, count):
    heads, rows, width = state.shape
    flat = rows * width
    lanes = 128
    vmem = pl.BlockSpec(memory_space=pltpu.VMEM)
    steps = max(1, (count - 1).bit_length())
    out_decay, out_state = pl.pallas_call(
        functools.partial(scan_kernel, count),
        out_shape=(
            jax.ShapeDtypeStruct((heads, lanes), jnp.float32),
            jax.ShapeDtypeStruct((heads, flat), jnp.float32),
        ),
        in_specs=[vmem, vmem],
        out_specs=(vmem, vmem),
        scratch_shapes=[
            pltpu.VMEM((steps, heads, flat + lanes), jnp.bfloat16),
            pltpu.VMEM((steps, heads, flat + lanes), jnp.bfloat16),
            pltpu.VMEM((heads, lanes), jnp.float32),
            pltpu.VMEM((heads, flat), jnp.float32),
            pltpu.SemaphoreType.DMA((steps,)),
            pltpu.SemaphoreType.DMA((steps,)),
        ],
        compiler_params=pltpu.CompilerParams(collective_id=0, has_side_effects=True),
    )(jnp.broadcast_to(decay[:, None], (heads, lanes)), state.reshape(heads, flat))
    return out_decay[:, 0], out_state.reshape(heads, rows, width)


def route_ranks(quarter_ids, experts):
    flattened = quarter_ids.reshape(-1)
    onehot = (flattened[:, None] == jnp.arange(experts, dtype=jnp.int32)[None, :]).astype(jnp.int32)
    running = jnp.cumsum(onehot, axis=0)
    rank_ids = jnp.sum(onehot * running, axis=1) - 1
    return (flattened, rank_ids)


def place_rows(normed, quarter_ids, experts, capacity):
    flattened, rank_ids = route_ranks(quarter_ids, experts)
    slot_ids = rank_ids * experts + flattened
    matches = (
        jnp.arange(capacity * experts, dtype=jnp.int32)[:, None] == slot_ids[None, :]
    ).astype(jnp.bfloat16)
    doubled = jnp.repeat(normed, quarter_ids.shape[1], axis=0)
    placed = jnp.dot(matches, doubled, preferred_element_type=jnp.float32).astype(jnp.bfloat16)
    return placed.reshape(capacity, experts, normed.shape[1])


def rms_rows(values, gain_vec):
    scaling = lax.rsqrt(jnp.mean(values * values, axis=1, keepdims=True) + eps_norm)
    return (values * scaling * gain_vec[None, :]).astype(jnp.bfloat16)


def local(
    inputs,
    gate_input,
    b_proj,
    c_proj,
    step_size,
    decay_rate,
    skip_gain,
    start_state,
    norm_gain,
    out_proj,
    residual,
    moe_gain,
    w_gate,
    w_up,
    w_down,
    route_ids,
    route_gates,
):
    tok_ctx = inputs.shape[0]
    head_count = step_size.shape[0]
    head_dim = inputs.shape[1] // head_count
    model_width = residual.shape[1]
    n_ctx = lax.axis_size("chip") * lax.axis_size("core")
    n_exp = lax.axis_size("exp")
    experts = n_ctx // PAIR
    tok_quarter = tok_ctx // n_exp
    capacity = 4 * tok_quarter // experts
    x_local = inputs.astype(jnp.float32).reshape(tok_ctx, head_count, head_dim)
    b_local = b_proj.astype(jnp.float32)
    c_local = c_proj.astype(jnp.float32)
    cumulative = jnp.cumsum(decay_rate, axis=1)
    span_total = cumulative[:, -1]
    sequence_indices = jnp.arange(tok_ctx, dtype=jnp.int32)
    causal = sequence_indices[:, None] >= sequence_indices[None, :]
    spread = jnp.where(causal[None], cumulative[:, :, None] - cumulative[:, None, :], 0.0)
    scores = jnp.dot(c_local, b_local.T, precision=top_precision)
    mixing = jnp.where(causal[None], jnp.exp(-spread), 0.0) * scores[None] * step_size[:, None, :]
    inside_part = jnp.einsum("hts,shp->thp", mixing, x_local, precision=top_precision)
    ending = jnp.exp(-(span_total[:, None] - cumulative)) * step_size
    local_state = jnp.einsum("hs,shp,sn->hpn", ending, x_local, b_local, precision=top_precision)
    prior_decay, prior_state = entering(jnp.exp(-span_total), local_state, n_ctx)
    incoming = prior_state + prior_decay[:, None, None] * start_state
    carried = (
        jnp.einsum("hpn,tn->thp", incoming, c_local, precision=top_precision)
        * jnp.exp(-cumulative).T[:, :, None]
    )
    ssm_out = inside_part + carried + skip_gain[None, :, None] * x_local
    gated_out = ssm_out.reshape(tok_ctx, head_count * head_dim) * jax.nn.silu(
        gate_input.astype(jnp.float32)
    )
    squares = jnp.sum(gated_out * gated_out, axis=1)
    unscaled_mix = (gated_out * norm_gain[None, :]).astype(jnp.bfloat16)
    partial_value = jnp.dot(
        unscaled_mix,
        lax.all_gather(out_proj, CTX, axis=1, tiled=True),
        preferred_element_type=jnp.float32,
    )
    width_out = partial_value.shape[1]
    joined = jnp.concatenate(
        [partial_value, jnp.broadcast_to(squares[:, None], (tok_ctx, 128))], axis=1
    ).astype(jnp.bfloat16)
    quarters = lax.all_to_all(
        joined.reshape(n_exp, tok_quarter, joined.shape[1]), "exp", split_axis=0, concat_axis=0, tiled=True
    )
    quarter_sum = jnp.sum(quarters.astype(jnp.float32), axis=0).astype(jnp.bfloat16)
    summed_parts = lax.all_to_all(
        jnp.broadcast_to(quarter_sum[None], (n_exp,) + quarter_sum.shape), "exp", split_axis=0, concat_axis=0, tiled=True
    ).reshape(tok_ctx, joined.shape[1]).astype(jnp.float32)
    scaling = lax.rsqrt(summed_parts[:, width_out] / (head_count * head_dim * n_exp) + eps_norm)
    mixed_all = summed_parts[:, :width_out] * scaling[:, None]
    gate_rows = w_gate[0]
    up_rows = w_up[0]
    down_rows = w_down[0]
    piece_width = gate_rows.shape[1]
    first_row = lax.axis_index("exp") * tok_quarter
    own_ids = lax.dynamic_slice_in_dim(route_ids, first_row, tok_quarter, 0)
    own_gates = lax.dynamic_slice_in_dim(route_gates, first_row, tok_quarter, 0)
    hidden_all = residual.astype(jnp.float32) + mixed_all
    moe_all = rms_rows(hidden_all, moe_gain)

    def place_quarter(quarter_rows, quarter_ids):
        return place_rows(quarter_rows, quarter_ids, experts, capacity)

    placed = jax.vmap(place_quarter)(
        moe_all.reshape(n_exp, tok_quarter, model_width),
        route_ids.reshape(n_exp, tok_quarter, route_ids.shape[1]),
    )
    placed = placed.reshape(n_exp * capacity, experts, model_width)
    swap = [(0, 1), (1, 0)]
    mine = lax.all_to_all(placed, "chip", split_axis=1, concat_axis=1, tiled=True)
    other = lax.ppermute(mine, "core", swap)
    hidden_own = lax.dynamic_slice_in_dim(hidden_all, first_row, tok_quarter, 0)

    def expert_rows(rows, by_permutes):
        flat = rows.reshape(-1, model_width)
        gate_val = jnp.dot(flat, gate_rows, preferred_element_type=jnp.float32)
        up_val = jnp.dot(flat, up_rows, preferred_element_type=jnp.float32)
        activated = (jax.nn.silu(gate_val) * up_val).astype(jnp.bfloat16)
        product = jnp.dot(activated, down_rows, preferred_element_type=jnp.float32)
        pieces = product.astype(jnp.bfloat16).reshape(rows.shape)
        if not by_permutes:
            return lax.psum_scatter(pieces, "exp", scatter_dimension=0, tiled=True)
        pieces = pieces.reshape((n_exp, capacity) + rows.shape[1:])
        place = lax.axis_index("exp")
        total = lax.dynamic_index_in_dim(pieces, place, 0, False).astype(jnp.float32)
        for shift in range(1, n_exp):
            outgoing = lax.dynamic_index_in_dim(pieces, (place + shift) % n_exp, 0, False)
            total = total + lax.ppermute(
                outgoing, "exp", [(i, (i + shift) % n_exp) for i in range(n_exp)]
            ).astype(jnp.float32)
        return total.astype(jnp.bfloat16)

    own_sum = expert_rows(mine, False)
    partner_sum = expert_rows(other, True)
    partner_half = lax.ppermute(partner_sum, "core", swap)
    both_halves = (own_sum.astype(jnp.float32) + partner_half.astype(jnp.float32)).astype(jnp.bfloat16)
    returned = lax.all_to_all(both_halves, "chip", split_axis=1, concat_axis=1, tiled=True)
    flattened, rank_ids = route_ranks(own_ids, experts)
    fetched = returned.reshape(capacity * experts, model_width)[rank_ids * experts + flattened]
    weighted = fetched.astype(jnp.float32) * own_gates.reshape(-1)[:, None]
    moe_out = jnp.sum(weighted.reshape(tok_quarter, -1, model_width), axis=1)
    return (hidden_own + moe_out).astype(jnp.bfloat16)


def solution(mesh):
    in_specs = (
        P(CTX, "exp"),
        P(CTX, "exp"),
        P(CTX, None),
        P(CTX, None),
        P("exp", CTX),
        P("exp", CTX),
        P("exp"),
        P("exp", None, None),
        P("exp"),
        P("exp", CTX),
        P(CTX, None),
        P(),
        P(CTX, None, "exp"),
        P(CTX, None, "exp"),
        P(CTX, "exp", None),
        P(CTX, None),
        P(CTX, None),
    )
    out_specs = P(("chip", "core", "exp"), None)
    split_mesh = Mesh(
        mesh.devices.reshape(mesh.devices.shape[0] // 2, 2, mesh.devices.shape[1]), ("chip", "core", "exp")
    )
    return jax.shard_map(local, mesh=split_mesh, in_specs=in_specs, out_specs=out_specs, check_vma=False)
```

```python
import functools

import jax
import jax.numpy as jnp
from jax import lax
from jax.experimental import pallas as pl
from jax.experimental.pallas import tpu as pltpu
from jax.sharding import Mesh, PartitionSpec as P

PAIR = 2
CTX = ("chip", "core")


eps_norm = 1e-05
top_precision = lax.Precision.HIGHEST


def scan_kernel(count, decay_ref, state_ref, out_decay, out_state, inc_buf, recv_buf,
                inc_decay, inc_state, send_sem, recv_sem):
    chip = lax.axis_index("chip")
    core = lax.axis_index("core")
    member = lax.axis_index("exp")
    place = chip * 2 + core
    width = state_ref.shape[1]
    hops = []
    hop = 1
    while hop < count:
        hops.append(hop)
        hop *= 2

    def target(index):
        return (index // 2, index % 2, member)

    barrier = pltpu.get_barrier_semaphore()
    partners = 0
    for hop in hops:
        ahead = place + hop < count
        behind = place >= hop
        partners = partners + ahead.astype(jnp.int32) + behind.astype(jnp.int32)

        @pl.when(ahead)
        def _():
            pl.semaphore_signal(barrier, inc=1, device_id=target(place + hop), device_id_type=pl.DeviceIdType.MESH)

        @pl.when(behind)
        def _():
            pl.semaphore_signal(barrier, inc=1, device_id=target(place - hop), device_id_type=pl.DeviceIdType.MESH)

    pl.semaphore_wait(barrier, partners)
    inc_decay[...] = decay_ref[...]
    inc_state[...] = state_ref[...]
    out_decay[...] = jnp.ones_like(out_decay)
    out_state[...] = jnp.zeros_like(out_state)
    for step, hop in enumerate(hops):
        ahead = place + hop < count
        behind = place >= hop
        inc_buf[step, :, :width] = inc_state[...].astype(jnp.bfloat16)
        inc_buf[step, :, width:] = inc_decay[...].astype(jnp.bfloat16)
        copy = pltpu.make_async_remote_copy(
            src_ref=inc_buf.at[step],
            dst_ref=recv_buf.at[step],
            send_sem=send_sem.at[step],
            recv_sem=recv_sem.at[step],
            device_id=target(jnp.minimum(place + hop, count - 1)),
            device_id_type=pl.DeviceIdType.MESH,
        )

        @pl.when(ahead)
        def _():
            copy.start()

        @pl.when(behind)
        def _():
            copy.wait_recv()
            got_state = recv_buf[step, :, :width].astype(jnp.float32)
            got_decay = recv_buf[step, :, width:].astype(jnp.float32)
            inc_state[...] = inc_decay[:, 0:1] * got_state + inc_state[...]
            inc_decay[...] = got_decay * inc_decay[...]
            out_state[...] = out_decay[:, 0:1] * got_state + out_state[...]
            out_decay[...] = got_decay * out_decay[...]

        @pl.when(ahead)
        def _():
            copy.wait_send()


def entering(decay, state, count):
    heads, rows, width = state.shape
    flat = rows * width
    lanes = 128
    vmem = pl.BlockSpec(memory_space=pltpu.VMEM)
    steps = max(1, (count - 1).bit_length())
    out_decay, out_state = pl.pallas_call(
        functools.partial(scan_kernel, count),
        out_shape=(
            jax.ShapeDtypeStruct((heads, lanes), jnp.float32),
            jax.ShapeDtypeStruct((heads, flat), jnp.float32),
        ),
        in_specs=[vmem, vmem],
        out_specs=(vmem, vmem),
        scratch_shapes=[
            pltpu.VMEM((steps, heads, flat + lanes), jnp.bfloat16),
            pltpu.VMEM((steps, heads, flat + lanes), jnp.bfloat16),
            pltpu.VMEM((heads, lanes), jnp.float32),
            pltpu.VMEM((heads, flat), jnp.float32),
            pltpu.SemaphoreType.DMA((steps,)),
            pltpu.SemaphoreType.DMA((steps,)),
        ],
        compiler_params=pltpu.CompilerParams(collective_id=0, has_side_effects=True),
    )(jnp.broadcast_to(decay[:, None], (heads, lanes)), state.reshape(heads, flat))
    return out_decay[:, 0], out_state.reshape(heads, rows, width)


def route_ranks(quarter_ids, experts):
    flattened = quarter_ids.reshape(-1)
    onehot = (flattened[:, None] == jnp.arange(experts, dtype=jnp.int32)[None, :]).astype(jnp.int32)
    running = jnp.cumsum(onehot, axis=0)
    rank_ids = jnp.sum(onehot * running, axis=1) - 1
    return (flattened, rank_ids)


def place_rows(normed, quarter_ids, experts, capacity):
    flattened, rank_ids = route_ranks(quarter_ids, experts)
    slot_ids = rank_ids * experts + flattened
    matches = (
        jnp.arange(capacity * experts, dtype=jnp.int32)[:, None] == slot_ids[None, :]
    ).astype(jnp.bfloat16)
    doubled = jnp.repeat(normed, quarter_ids.shape[1], axis=0)
    placed = jnp.dot(matches, doubled, preferred_element_type=jnp.float32).astype(jnp.bfloat16)
    return placed.reshape(capacity, experts, normed.shape[1])


def rms_rows(values, gain_vec):
    scaling = lax.rsqrt(jnp.mean(values * values, axis=1, keepdims=True) + eps_norm)
    return (values * scaling * gain_vec[None, :]).astype(jnp.bfloat16)


def local(
    inputs,
    gate_input,
    b_proj,
    c_proj,
    step_size,
    decay_rate,
    skip_gain,
    start_state,
    norm_gain,
    out_proj,
    residual,
    moe_gain,
    w_gate,
    w_up,
    w_down,
    route_ids,
    route_gates,
):
    tok_ctx = inputs.shape[0]
    head_count = step_size.shape[0]
    head_dim = inputs.shape[1] // head_count
    model_width = residual.shape[1]
    n_ctx = lax.axis_size("chip") * lax.axis_size("core")
    n_exp = lax.axis_size("exp")
    experts = n_ctx // PAIR
    tok_quarter = tok_ctx // n_exp
    capacity = 4 * tok_quarter // experts
    x_local = inputs.astype(jnp.float32).reshape(tok_ctx, head_count, head_dim)
    b_local = b_proj.astype(jnp.float32)
    c_local = c_proj.astype(jnp.float32)
    cumulative = jnp.cumsum(decay_rate, axis=1)
    span_total = cumulative[:, -1]
    sequence_indices = jnp.arange(tok_ctx, dtype=jnp.int32)
    causal = sequence_indices[:, None] >= sequence_indices[None, :]
    spread = jnp.where(causal[None], cumulative[:, :, None] - cumulative[:, None, :], 0.0)
    scores = jnp.dot(c_local, b_local.T, precision=top_precision)
    mixing = jnp.where(causal[None], jnp.exp(-spread), 0.0) * scores[None] * step_size[:, None, :]
    inside_part = jnp.einsum("hts,shp->thp", mixing, x_local, precision=top_precision)
    ending = jnp.exp(-(span_total[:, None] - cumulative)) * step_size
    local_state = jnp.einsum("hs,shp,sn->hpn", ending, x_local, b_local, precision=top_precision)
    prior_decay, prior_state = entering(jnp.exp(-span_total), local_state, n_ctx)
    incoming = prior_state + prior_decay[:, None, None] * start_state
    carried = (
        jnp.einsum("hpn,tn->thp", incoming, c_local, precision=top_precision)
        * jnp.exp(-cumulative).T[:, :, None]
    )
    ssm_out = inside_part + carried + skip_gain[None, :, None] * x_local
    gated_out = ssm_out.reshape(tok_ctx, head_count * head_dim) * jax.nn.silu(
        gate_input.astype(jnp.float32)
    )
    squares = jnp.sum(gated_out * gated_out, axis=1)
    unscaled_mix = (gated_out * norm_gain[None, :]).astype(jnp.bfloat16)
    partial_value = jnp.dot(
        unscaled_mix,
        lax.all_gather(out_proj, CTX, axis=1, tiled=True),
        preferred_element_type=jnp.float32,
    )
    width_out = partial_value.shape[1]
    joined = jnp.concatenate(
        [partial_value, jnp.broadcast_to(squares[:, None], (tok_ctx, 128))], axis=1
    ).astype(jnp.bfloat16)
    quarters = lax.all_to_all(
        joined.reshape(n_exp, tok_quarter, joined.shape[1]), "exp", split_axis=0, concat_axis=0, tiled=True
    )
    quarter_sum = jnp.sum(quarters.astype(jnp.float32), axis=0).astype(jnp.bfloat16)
    summed_parts = lax.all_to_all(
        jnp.broadcast_to(quarter_sum[None], (n_exp,) + quarter_sum.shape), "exp", split_axis=0, concat_axis=0, tiled=True
    ).reshape(tok_ctx, joined.shape[1]).astype(jnp.float32)
    scaling = lax.rsqrt(summed_parts[:, width_out] / (head_count * head_dim * n_exp) + eps_norm)
    mixed_all = summed_parts[:, :width_out] * scaling[:, None]
    gate_rows = w_gate[0]
    up_rows = w_up[0]
    down_rows = w_down[0]
    piece_width = gate_rows.shape[1]
    first_row = lax.axis_index("exp") * tok_quarter
    own_ids = lax.dynamic_slice_in_dim(route_ids, first_row, tok_quarter, 0)
    own_gates = lax.dynamic_slice_in_dim(route_gates, first_row, tok_quarter, 0)
    hidden_all = residual.astype(jnp.float32) + mixed_all
    moe_all = rms_rows(hidden_all, moe_gain)

    def place_quarter(quarter_rows, quarter_ids):
        return place_rows(quarter_rows, quarter_ids, experts, capacity)

    placed = jax.vmap(place_quarter)(
        moe_all.reshape(n_exp, tok_quarter, model_width),
        route_ids.reshape(n_exp, tok_quarter, route_ids.shape[1]),
    )
    placed = placed.reshape(n_exp * capacity, experts, model_width)
    swap = [(0, 1), (1, 0)]
    mine = lax.all_to_all(placed, "chip", split_axis=1, concat_axis=1, tiled=True)
    other = lax.ppermute(mine, "core", swap)
    hidden_own = lax.dynamic_slice_in_dim(hidden_all, first_row, tok_quarter, 0)

    def expert_rows(rows, by_permutes):
        flat = rows.reshape(-1, model_width)
        gate_val = jnp.dot(flat, gate_rows, preferred_element_type=jnp.float32)
        up_val = jnp.dot(flat, up_rows, preferred_element_type=jnp.float32)
        activated = (jax.nn.silu(gate_val) * up_val).astype(jnp.bfloat16)
        product = jnp.dot(activated, down_rows, preferred_element_type=jnp.float32)
        pieces = product.astype(jnp.bfloat16).reshape(rows.shape)
        if not by_permutes:
            return lax.psum_scatter(pieces, "exp", scatter_dimension=0, tiled=True)
        pieces = pieces.reshape((n_exp, capacity) + rows.shape[1:])
        place = lax.axis_index("exp")
        total = lax.dynamic_index_in_dim(pieces, place, 0, False).astype(jnp.float32)
        for shift in range(1, n_exp):
            outgoing = lax.dynamic_index_in_dim(pieces, (place + shift) % n_exp, 0, False)
            total = total + lax.ppermute(
                outgoing, "exp", [(i, (i + shift) % n_exp) for i in range(n_exp)]
            ).astype(jnp.float32)
        return total.astype(jnp.bfloat16)

    own_sum = expert_rows(mine, True)
    partner_sum = expert_rows(other, False)
    partner_half = lax.ppermute(partner_sum, "core", swap)
    both_halves = (own_sum.astype(jnp.float32) + partner_half.astype(jnp.float32)).astype(jnp.bfloat16)
    returned = lax.all_to_all(both_halves, "chip", split_axis=1, concat_axis=1, tiled=True)
    flattened, rank_ids = route_ranks(own_ids, experts)
    fetched = returned.reshape(capacity * experts, model_width)[rank_ids * experts + flattened]
    weighted = fetched.astype(jnp.float32) * own_gates.reshape(-1)[:, None]
    moe_out = jnp.sum(weighted.reshape(tok_quarter, -1, model_width), axis=1)
    return (hidden_own + moe_out).astype(jnp.bfloat16)


def solution(mesh):
    in_specs = (
        P(CTX, "exp"),
        P(CTX, "exp"),
        P(CTX, None),
        P(CTX, None),
        P("exp", CTX),
        P("exp", CTX),
        P("exp"),
        P("exp", None, None),
        P("exp"),
        P("exp", CTX),
        P(CTX, None),
        P(),
        P(CTX, None, "exp"),
        P(CTX, None, "exp"),
        P(CTX, "exp", None),
        P(CTX, None),
        P(CTX, None),
    )
    out_specs = P(("chip", "core", "exp"), None)
    split_mesh = Mesh(
        mesh.devices.reshape(mesh.devices.shape[0] // 2, 2, mesh.devices.shape[1]), ("chip", "core", "exp")
    )
    return jax.shard_map(local, mesh=split_mesh, in_specs=in_specs, out_specs=out_specs, check_vma=False)
```

```python
import functools

import jax
import jax.numpy as jnp
from jax import lax
from jax.experimental import pallas as pl
from jax.experimental.pallas import tpu as pltpu
from jax.sharding import Mesh, PartitionSpec as P

PAIR = 2
CTX = ("chip", "core")


eps_norm = 1e-05
top_precision = lax.Precision.HIGHEST


def scan_kernel(count, decay_ref, state_ref, out_decay, out_state, inc_buf, recv_buf,
                inc_decay, inc_state, send_sem, recv_sem):
    chip = lax.axis_index("chip")
    core = lax.axis_index("core")
    member = lax.axis_index("exp")
    place = chip * 2 + core
    width = state_ref.shape[1]
    hops = []
    hop = 1
    while hop < count:
        hops.append(hop)
        hop *= 2

    def target(index):
        return (index // 2, index % 2, member)

    barrier = pltpu.get_barrier_semaphore()
    partners = 0
    for hop in hops:
        ahead = place + hop < count
        behind = place >= hop
        partners = partners + ahead.astype(jnp.int32) + behind.astype(jnp.int32)

        @pl.when(ahead)
        def _():
            pl.semaphore_signal(barrier, inc=1, device_id=target(place + hop), device_id_type=pl.DeviceIdType.MESH)

        @pl.when(behind)
        def _():
            pl.semaphore_signal(barrier, inc=1, device_id=target(place - hop), device_id_type=pl.DeviceIdType.MESH)

    pl.semaphore_wait(barrier, partners)
    inc_decay[...] = decay_ref[...]
    inc_state[...] = state_ref[...]
    out_decay[...] = jnp.ones_like(out_decay)
    out_state[...] = jnp.zeros_like(out_state)
    for step, hop in enumerate(hops):
        ahead = place + hop < count
        behind = place >= hop
        inc_buf[step, :, :width] = inc_state[...].astype(jnp.bfloat16)
        inc_buf[step, :, width:] = inc_decay[...].astype(jnp.bfloat16)
        copy = pltpu.make_async_remote_copy(
            src_ref=inc_buf.at[step],
            dst_ref=recv_buf.at[step],
            send_sem=send_sem.at[step],
            recv_sem=recv_sem.at[step],
            device_id=target(jnp.minimum(place + hop, count - 1)),
            device_id_type=pl.DeviceIdType.MESH,
        )

        @pl.when(ahead)
        def _():
            copy.start()

        @pl.when(behind)
        def _():
            copy.wait_recv()
            got_state = recv_buf[step, :, :width].astype(jnp.float32)
            got_decay = recv_buf[step, :, width:].astype(jnp.float32)
            inc_state[...] = inc_decay[:, 0:1] * got_state + inc_state[...]
            inc_decay[...] = got_decay * inc_decay[...]
            out_state[...] = out_decay[:, 0:1] * got_state + out_state[...]
            out_decay[...] = got_decay * out_decay[...]

        @pl.when(ahead)
        def _():
            copy.wait_send()


def entering(decay, state, count):
    heads, rows, width = state.shape
    flat = rows * width
    lanes = 128
    vmem = pl.BlockSpec(memory_space=pltpu.VMEM)
    steps = max(1, (count - 1).bit_length())
    out_decay, out_state = pl.pallas_call(
        functools.partial(scan_kernel, count),
        out_shape=(
            jax.ShapeDtypeStruct((heads, lanes), jnp.float32),
            jax.ShapeDtypeStruct((heads, flat), jnp.float32),
        ),
        in_specs=[vmem, vmem],
        out_specs=(vmem, vmem),
        scratch_shapes=[
            pltpu.VMEM((steps, heads, flat + lanes), jnp.bfloat16),
            pltpu.VMEM((steps, heads, flat + lanes), jnp.bfloat16),
            pltpu.VMEM((heads, lanes), jnp.float32),
            pltpu.VMEM((heads, flat), jnp.float32),
            pltpu.SemaphoreType.DMA((steps,)),
            pltpu.SemaphoreType.DMA((steps,)),
        ],
        compiler_params=pltpu.CompilerParams(collective_id=0, has_side_effects=True),
    )(jnp.broadcast_to(decay[:, None], (heads, lanes)), state.reshape(heads, flat))
    return out_decay[:, 0], out_state.reshape(heads, rows, width)


def route_ranks(quarter_ids, experts):
    flattened = quarter_ids.reshape(-1)
    onehot = (flattened[:, None] == jnp.arange(experts, dtype=jnp.int32)[None, :]).astype(jnp.int32)
    running = jnp.cumsum(onehot, axis=0)
    rank_ids = jnp.sum(onehot * running, axis=1) - 1
    return (flattened, rank_ids)


def place_rows(normed, quarter_ids, experts, capacity):
    flattened, rank_ids = route_ranks(quarter_ids, experts)
    slot_ids = rank_ids * experts + flattened
    matches = (
        jnp.arange(capacity * experts, dtype=jnp.int32)[:, None] == slot_ids[None, :]
    ).astype(jnp.bfloat16)
    doubled = jnp.repeat(normed, quarter_ids.shape[1], axis=0)
    placed = jnp.dot(matches, doubled, preferred_element_type=jnp.float32).astype(jnp.bfloat16)
    return placed.reshape(capacity, experts, normed.shape[1])


def rms_rows(values, gain_vec):
    scaling = lax.rsqrt(jnp.mean(values * values, axis=1, keepdims=True) + eps_norm)
    return (values * scaling * gain_vec[None, :]).astype(jnp.bfloat16)


def local(
    inputs,
    gate_input,
    b_proj,
    c_proj,
    step_size,
    decay_rate,
    skip_gain,
    start_state,
    norm_gain,
    out_proj,
    residual,
    moe_gain,
    w_gate,
    w_up,
    w_down,
    route_ids,
    route_gates,
):
    tok_ctx = inputs.shape[0]
    head_count = step_size.shape[0]
    head_dim = inputs.shape[1] // head_count
    model_width = residual.shape[1]
    n_ctx = lax.axis_size("chip") * lax.axis_size("core")
    n_exp = lax.axis_size("exp")
    experts = n_ctx // PAIR
    tok_quarter = tok_ctx // n_exp
    capacity = 4 * tok_quarter // experts
    x_local = inputs.astype(jnp.float32).reshape(tok_ctx, head_count, head_dim)
    b_local = b_proj.astype(jnp.float32)
    c_local = c_proj.astype(jnp.float32)
    cumulative = jnp.cumsum(decay_rate, axis=1)
    span_total = cumulative[:, -1]
    sequence_indices = jnp.arange(tok_ctx, dtype=jnp.int32)
    causal = sequence_indices[:, None] >= sequence_indices[None, :]
    spread = jnp.where(causal[None], cumulative[:, :, None] - cumulative[:, None, :], 0.0)
    scores = jnp.dot(c_local, b_local.T, precision=top_precision)
    mixing = jnp.where(causal[None], jnp.exp(-spread), 0.0) * scores[None] * step_size[:, None, :]
    inside_part = jnp.einsum("hts,shp->thp", mixing, x_local, precision=top_precision)
    ending = jnp.exp(-(span_total[:, None] - cumulative)) * step_size
    local_state = jnp.einsum("hs,shp,sn->hpn", ending, x_local, b_local, precision=top_precision)
    prior_decay, prior_state = entering(jnp.exp(-span_total), local_state, n_ctx)
    incoming = prior_state + prior_decay[:, None, None] * start_state
    carried = (
        jnp.einsum("hpn,tn->thp", incoming, c_local, precision=top_precision)
        * jnp.exp(-cumulative).T[:, :, None]
    )
    ssm_out = inside_part + carried + skip_gain[None, :, None] * x_local
    gated_out = ssm_out.reshape(tok_ctx, head_count * head_dim) * jax.nn.silu(
        gate_input.astype(jnp.float32)
    )
    squares = jnp.sum(gated_out * gated_out, axis=1)
    unscaled_mix = (gated_out * norm_gain[None, :]).astype(jnp.bfloat16)
    partial_value = jnp.dot(
        unscaled_mix,
        lax.all_gather(out_proj, CTX, axis=1, tiled=True),
        preferred_element_type=jnp.float32,
    )
    width_out = partial_value.shape[1]
    joined = jnp.concatenate(
        [partial_value, jnp.broadcast_to(squares[:, None], (tok_ctx, 128))], axis=1
    ).astype(jnp.bfloat16)
    quarters = lax.all_to_all(
        joined.reshape(n_exp, tok_quarter, joined.shape[1]), "exp", split_axis=0, concat_axis=0, tiled=True
    )
    quarter_sum = jnp.sum(quarters.astype(jnp.float32), axis=0).astype(jnp.bfloat16)
    own_parts = quarter_sum.astype(jnp.float32)
    scaling = lax.rsqrt(own_parts[:, width_out] / (head_count * head_dim * n_exp) + eps_norm)
    mixed_own = own_parts[:, :width_out] * scaling[:, None]
    gate_rows = w_gate[0]
    up_rows = w_up[0]
    down_rows = w_down[0]
    piece_width = gate_rows.shape[1]
    first_row = lax.axis_index("exp") * tok_quarter
    own_ids = lax.dynamic_slice_in_dim(route_ids, first_row, tok_quarter, 0)
    own_gates = lax.dynamic_slice_in_dim(route_gates, first_row, tok_quarter, 0)
    own_residual = lax.dynamic_slice_in_dim(residual, first_row, tok_quarter, 0)
    hidden_own = own_residual.astype(jnp.float32) + mixed_own
    moe_own = rms_rows(hidden_own, moe_gain)
    moe_all = lax.all_to_all(
        jnp.broadcast_to(moe_own[None], (n_exp,) + moe_own.shape), "exp", split_axis=0, concat_axis=0, tiled=True
    ).reshape(tok_ctx, model_width)

    def place_quarter(quarter_rows, quarter_ids):
        return place_rows(quarter_rows, quarter_ids, experts, capacity)

    placed = jax.vmap(place_quarter)(
        moe_all.reshape(n_exp, tok_quarter, model_width),
        route_ids.reshape(n_exp, tok_quarter, route_ids.shape[1]),
    )
    placed = placed.reshape(n_exp * capacity, experts, model_width)
    swap = [(0, 1), (1, 0)]
    mine = lax.all_to_all(placed, "chip", split_axis=1, concat_axis=1, tiled=True)
    other = lax.ppermute(mine, "core", swap)

    def expert_rows(rows, by_permutes):
        flat = rows.reshape(-1, model_width)
        gate_val = jnp.dot(flat, gate_rows, preferred_element_type=jnp.float32)
        up_val = jnp.dot(flat, up_rows, preferred_element_type=jnp.float32)
        activated = (jax.nn.silu(gate_val) * up_val).astype(jnp.bfloat16)
        product = jnp.dot(activated, down_rows, preferred_element_type=jnp.float32)
        pieces = product.astype(jnp.bfloat16).reshape(rows.shape)
        if not by_permutes:
            return lax.psum_scatter(pieces, "exp", scatter_dimension=0, tiled=True)
        pieces = pieces.reshape((n_exp, capacity) + rows.shape[1:])
        place = lax.axis_index("exp")
        total = lax.dynamic_index_in_dim(pieces, place, 0, False).astype(jnp.float32)
        for shift in range(1, n_exp):
            outgoing = lax.dynamic_index_in_dim(pieces, (place + shift) % n_exp, 0, False)
            total = total + lax.ppermute(
                outgoing, "exp", [(i, (i + shift) % n_exp) for i in range(n_exp)]
            ).astype(jnp.float32)
        return total.astype(jnp.bfloat16)

    own_sum = expert_rows(mine, False)
    partner_sum = expert_rows(other, True)
    partner_half = lax.ppermute(partner_sum, "core", swap)
    both_halves = (own_sum.astype(jnp.float32) + partner_half.astype(jnp.float32)).astype(jnp.bfloat16)
    returned = lax.all_to_all(both_halves, "chip", split_axis=1, concat_axis=1, tiled=True)
    flattened, rank_ids = route_ranks(own_ids, experts)
    fetched = returned.reshape(capacity * experts, model_width)[rank_ids * experts + flattened]
    weighted = fetched.astype(jnp.float32) * own_gates.reshape(-1)[:, None]
    moe_out = jnp.sum(weighted.reshape(tok_quarter, -1, model_width), axis=1)
    return (hidden_own + moe_out).astype(jnp.bfloat16)


def solution(mesh):
    in_specs = (
        P(CTX, "exp"),
        P(CTX, "exp"),
        P(CTX, None),
        P(CTX, None),
        P("exp", CTX),
        P("exp", CTX),
        P("exp"),
        P("exp", None, None),
        P("exp"),
        P("exp", CTX),
        P(CTX, None),
        P(),
        P(CTX, None, "exp"),
        P(CTX, None, "exp"),
        P(CTX, "exp", None),
        P(CTX, None),
        P(CTX, None),
    )
    out_specs = P(("chip", "core", "exp"), None)
    split_mesh = Mesh(
        mesh.devices.reshape(mesh.devices.shape[0] // 2, 2, mesh.devices.shape[1]), ("chip", "core", "exp")
    )
    return jax.shard_map(local, mesh=split_mesh, in_specs=in_specs, out_specs=out_specs, check_vma=False)
```

```python
import functools

import jax
import jax.numpy as jnp
from jax import lax
from jax.experimental import pallas as pl
from jax.experimental.pallas import tpu as pltpu
from jax.sharding import Mesh, PartitionSpec as P

PAIR = 2
CTX = ("chip", "core")


eps_norm = 1e-05
top_precision = lax.Precision.HIGHEST


def scan_kernel(count, decay_ref, state_ref, out_decay, out_state, inc_buf, recv_buf,
                inc_decay, inc_state, send_sem, recv_sem):
    chip = lax.axis_index("chip")
    core = lax.axis_index("core")
    member = lax.axis_index("exp")
    place = chip * 2 + core
    width = state_ref.shape[1]
    hops = []
    hop = 1
    while hop < count:
        hops.append(hop)
        hop *= 2

    def target(index):
        return (index // 2, index % 2, member)

    barrier = pltpu.get_barrier_semaphore()
    partners = 0
    for hop in hops:
        ahead = place + hop < count
        behind = place >= hop
        partners = partners + ahead.astype(jnp.int32) + behind.astype(jnp.int32)

        @pl.when(ahead)
        def _():
            pl.semaphore_signal(barrier, inc=1, device_id=target(place + hop), device_id_type=pl.DeviceIdType.MESH)

        @pl.when(behind)
        def _():
            pl.semaphore_signal(barrier, inc=1, device_id=target(place - hop), device_id_type=pl.DeviceIdType.MESH)

    pl.semaphore_wait(barrier, partners)
    inc_decay[...] = decay_ref[...]
    inc_state[...] = state_ref[...]
    out_decay[...] = jnp.ones_like(out_decay)
    out_state[...] = jnp.zeros_like(out_state)
    for step, hop in enumerate(hops):
        ahead = place + hop < count
        behind = place >= hop
        inc_buf[step, :, :width] = inc_state[...].astype(jnp.bfloat16)
        inc_buf[step, :, width:] = inc_decay[...].astype(jnp.bfloat16)
        copy = pltpu.make_async_remote_copy(
            src_ref=inc_buf.at[step],
            dst_ref=recv_buf.at[step],
            send_sem=send_sem.at[step],
            recv_sem=recv_sem.at[step],
            device_id=target(jnp.minimum(place + hop, count - 1)),
            device_id_type=pl.DeviceIdType.MESH,
        )

        @pl.when(ahead)
        def _():
            copy.start()

        @pl.when(behind)
        def _():
            copy.wait_recv()
            got_state = recv_buf[step, :, :width].astype(jnp.float32)
            got_decay = recv_buf[step, :, width:].astype(jnp.float32)
            inc_state[...] = inc_decay[:, 0:1] * got_state + inc_state[...]
            inc_decay[...] = got_decay * inc_decay[...]
            out_state[...] = out_decay[:, 0:1] * got_state + out_state[...]
            out_decay[...] = got_decay * out_decay[...]

        @pl.when(ahead)
        def _():
            copy.wait_send()


def entering(decay, state, count):
    heads, rows, width = state.shape
    flat = rows * width
    lanes = 128
    vmem = pl.BlockSpec(memory_space=pltpu.VMEM)
    steps = max(1, (count - 1).bit_length())
    out_decay, out_state = pl.pallas_call(
        functools.partial(scan_kernel, count),
        out_shape=(
            jax.ShapeDtypeStruct((heads, lanes), jnp.float32),
            jax.ShapeDtypeStruct((heads, flat), jnp.float32),
        ),
        in_specs=[vmem, vmem],
        out_specs=(vmem, vmem),
        scratch_shapes=[
            pltpu.VMEM((steps, heads, flat + lanes), jnp.bfloat16),
            pltpu.VMEM((steps, heads, flat + lanes), jnp.bfloat16),
            pltpu.VMEM((heads, lanes), jnp.float32),
            pltpu.VMEM((heads, flat), jnp.float32),
            pltpu.SemaphoreType.DMA((steps,)),
            pltpu.SemaphoreType.DMA((steps,)),
        ],
        compiler_params=pltpu.CompilerParams(collective_id=0, has_side_effects=True),
    )(jnp.broadcast_to(decay[:, None], (heads, lanes)), state.reshape(heads, flat))
    return out_decay[:, 0], out_state.reshape(heads, rows, width)


def route_ranks(quarter_ids, experts):
    flattened = quarter_ids.reshape(-1)
    onehot = (flattened[:, None] == jnp.arange(experts, dtype=jnp.int32)[None, :]).astype(jnp.int32)
    running = jnp.cumsum(onehot, axis=0)
    rank_ids = jnp.sum(onehot * running, axis=1) - 1
    return (flattened, rank_ids)


def place_rows(normed, quarter_ids, experts, capacity):
    flattened, rank_ids = route_ranks(quarter_ids, experts)
    slot_ids = rank_ids * experts + flattened
    matches = (
        jnp.arange(capacity * experts, dtype=jnp.int32)[:, None] == slot_ids[None, :]
    ).astype(jnp.bfloat16)
    doubled = jnp.repeat(normed, quarter_ids.shape[1], axis=0)
    placed = jnp.dot(matches, doubled, preferred_element_type=jnp.float32).astype(jnp.bfloat16)
    return placed.reshape(capacity, experts, normed.shape[1])


def rms_rows(values, gain_vec):
    scaling = lax.rsqrt(jnp.mean(values * values, axis=1, keepdims=True) + eps_norm)
    return (values * scaling * gain_vec[None, :]).astype(jnp.bfloat16)


def local(
    inputs,
    gate_input,
    b_proj,
    c_proj,
    step_size,
    decay_rate,
    skip_gain,
    start_state,
    norm_gain,
    out_proj,
    residual,
    moe_gain,
    w_gate,
    w_up,
    w_down,
    route_ids,
    route_gates,
):
    tok_ctx = inputs.shape[0]
    head_count = step_size.shape[0]
    head_dim = inputs.shape[1] // head_count
    model_width = residual.shape[1]
    n_ctx = lax.axis_size("chip") * lax.axis_size("core")
    n_exp = lax.axis_size("exp")
    experts = n_ctx // PAIR
    tok_quarter = tok_ctx // n_exp
    capacity = 4 * tok_quarter // experts
    x_local = inputs.astype(jnp.float32).reshape(tok_ctx, head_count, head_dim)
    b_local = b_proj.astype(jnp.float32)
    c_local = c_proj.astype(jnp.float32)
    cumulative = jnp.cumsum(decay_rate, axis=1)
    span_total = cumulative[:, -1]
    sequence_indices = jnp.arange(tok_ctx, dtype=jnp.int32)
    causal = sequence_indices[:, None] >= sequence_indices[None, :]
    spread = jnp.where(causal[None], cumulative[:, :, None] - cumulative[:, None, :], 0.0)
    scores = jnp.dot(c_local, b_local.T, precision=top_precision)
    mixing = jnp.where(causal[None], jnp.exp(-spread), 0.0) * scores[None] * step_size[:, None, :]
    inside_part = jnp.einsum("hts,shp->thp", mixing, x_local, precision=top_precision)
    ending = jnp.exp(-(span_total[:, None] - cumulative)) * step_size
    local_state = jnp.einsum("hs,shp,sn->hpn", ending, x_local, b_local, precision=top_precision)
    prior_decay, prior_state = entering(jnp.exp(-span_total), local_state, n_ctx)
    incoming = prior_state + prior_decay[:, None, None] * start_state
    carried = (
        jnp.einsum("hpn,tn->thp", incoming, c_local, precision=top_precision)
        * jnp.exp(-cumulative).T[:, :, None]
    )
    ssm_out = inside_part + carried + skip_gain[None, :, None] * x_local
    gated_out = ssm_out.reshape(tok_ctx, head_count * head_dim) * jax.nn.silu(
        gate_input.astype(jnp.float32)
    )
    squares = jnp.sum(gated_out * gated_out, axis=1)
    unscaled_mix = (gated_out * norm_gain[None, :]).astype(jnp.bfloat16)
    partial_value = jnp.dot(
        unscaled_mix,
        lax.all_gather(out_proj, CTX, axis=1, tiled=True),
        preferred_element_type=jnp.float32,
    )
    width_out = partial_value.shape[1]
    joined = jnp.concatenate(
        [partial_value, jnp.broadcast_to(squares[:, None], (tok_ctx, 128))], axis=1
    ).astype(jnp.bfloat16)
    quarters = lax.all_to_all(
        joined.reshape(n_exp, tok_quarter, joined.shape[1]), "exp", split_axis=0, concat_axis=0, tiled=True
    )
    quarter_sum = jnp.sum(quarters.astype(jnp.float32), axis=0).astype(jnp.bfloat16)
    own_parts = quarter_sum.astype(jnp.float32)
    scaling = lax.rsqrt(own_parts[:, width_out] / (head_count * head_dim * n_exp) + eps_norm)
    mixed_own = own_parts[:, :width_out] * scaling[:, None]
    gate_rows = w_gate[0]
    up_rows = w_up[0]
    down_rows = w_down[0]
    piece_width = gate_rows.shape[1]
    first_row = lax.axis_index("exp") * tok_quarter
    own_ids = lax.dynamic_slice_in_dim(route_ids, first_row, tok_quarter, 0)
    own_gates = lax.dynamic_slice_in_dim(route_gates, first_row, tok_quarter, 0)
    own_residual = lax.dynamic_slice_in_dim(residual, first_row, tok_quarter, 0)
    hidden_own = own_residual.astype(jnp.float32) + mixed_own
    moe_own = rms_rows(hidden_own, moe_gain)
    moe_all = lax.all_to_all(
        jnp.broadcast_to(moe_own[None], (n_exp,) + moe_own.shape), "exp", split_axis=0, concat_axis=0, tiled=True
    ).reshape(tok_ctx, model_width)

    def place_quarter(quarter_rows, quarter_ids):
        return place_rows(quarter_rows, quarter_ids, experts, capacity)

    placed = jax.vmap(place_quarter)(
        moe_all.reshape(n_exp, tok_quarter, model_width),
        route_ids.reshape(n_exp, tok_quarter, route_ids.shape[1]),
    )
    placed = placed.reshape(n_exp * capacity, experts, model_width)
    swap = [(0, 1), (1, 0)]
    mine = lax.all_to_all(placed, "chip", split_axis=1, concat_axis=1, tiled=True)
    other = lax.ppermute(mine, "core", swap)

    def expert_rows(rows, by_permutes):
        flat = rows.reshape(-1, model_width)
        gate_val = jnp.dot(flat, gate_rows, preferred_element_type=jnp.float32)
        up_val = jnp.dot(flat, up_rows, preferred_element_type=jnp.float32)
        activated = (jax.nn.silu(gate_val) * up_val).astype(jnp.bfloat16)
        product = jnp.dot(activated, down_rows, preferred_element_type=jnp.float32)
        pieces = product.astype(jnp.bfloat16).reshape(rows.shape)
        if not by_permutes:
            return lax.psum_scatter(pieces, "exp", scatter_dimension=0, tiled=True)
        split = rows.shape[1] // 2
        by_call = lax.psum_scatter(pieces[:, :split], "exp", scatter_dimension=0, tiled=True)
        pieces = pieces[:, split:].reshape((n_exp, capacity, rows.shape[1] - split) + rows.shape[2:])
        place = lax.axis_index("exp")
        total = lax.dynamic_index_in_dim(pieces, place, 0, False).astype(jnp.float32)
        for shift in range(1, n_exp):
            outgoing = lax.dynamic_index_in_dim(pieces, (place + shift) % n_exp, 0, False)
            total = total + lax.ppermute(
                outgoing, "exp", [(i, (i + shift) % n_exp) for i in range(n_exp)]
            ).astype(jnp.float32)
        return jnp.concatenate([by_call, total.astype(jnp.bfloat16)], axis=1)

    own_sum = expert_rows(mine, False)
    partner_sum = expert_rows(other, True)
    partner_half = lax.ppermute(partner_sum, "core", swap)
    both_halves = (own_sum.astype(jnp.float32) + partner_half.astype(jnp.float32)).astype(jnp.bfloat16)
    returned = lax.all_to_all(both_halves, "chip", split_axis=1, concat_axis=1, tiled=True)
    flattened, rank_ids = route_ranks(own_ids, experts)
    fetched = returned.reshape(capacity * experts, model_width)[rank_ids * experts + flattened]
    weighted = fetched.astype(jnp.float32) * own_gates.reshape(-1)[:, None]
    moe_out = jnp.sum(weighted.reshape(tok_quarter, -1, model_width), axis=1)
    return (hidden_own + moe_out).astype(jnp.bfloat16)


def solution(mesh):
    in_specs = (
        P(CTX, "exp"),
        P(CTX, "exp"),
        P(CTX, None),
        P(CTX, None),
        P("exp", CTX),
        P("exp", CTX),
        P("exp"),
        P("exp", None, None),
        P("exp"),
        P("exp", CTX),
        P(CTX, None),
        P(),
        P(CTX, None, "exp"),
        P(CTX, None, "exp"),
        P(CTX, "exp", None),
        P(CTX, None),
        P(CTX, None),
    )
    out_specs = P(("chip", "core", "exp"), None)
    split_mesh = Mesh(
        mesh.devices.reshape(mesh.devices.shape[0] // 2, 2, mesh.devices.shape[1]), ("chip", "core", "exp")
    )
    return jax.shard_map(local, mesh=split_mesh, in_specs=in_specs, out_specs=out_specs, check_vma=False)
```

```python
import functools

import jax
import jax.numpy as jnp
from jax import lax
from jax.experimental import pallas as pl
from jax.experimental.pallas import tpu as pltpu
from jax.sharding import Mesh, PartitionSpec as P

PAIR = 2
CTX = ("chip", "core")


eps_norm = 1e-05
top_precision = lax.Precision.HIGHEST


def scan_kernel(count, decay_ref, state_ref, out_decay, out_state, inc_buf, recv_buf,
                inc_decay, inc_state, send_sem, recv_sem):
    chip = lax.axis_index("chip")
    core = lax.axis_index("core")
    member = lax.axis_index("exp")
    place = chip * 2 + core
    width = state_ref.shape[1]
    hops = []
    hop = 1
    while hop < count:
        hops.append(hop)
        hop *= 2

    def target(index):
        return (index // 2, index % 2, member)

    barrier = pltpu.get_barrier_semaphore()
    partners = 0
    for hop in hops:
        ahead = place + hop < count
        behind = place >= hop
        partners = partners + ahead.astype(jnp.int32) + behind.astype(jnp.int32)

        @pl.when(ahead)
        def _():
            pl.semaphore_signal(barrier, inc=1, device_id=target(place + hop), device_id_type=pl.DeviceIdType.MESH)

        @pl.when(behind)
        def _():
            pl.semaphore_signal(barrier, inc=1, device_id=target(place - hop), device_id_type=pl.DeviceIdType.MESH)

    pl.semaphore_wait(barrier, partners)
    inc_decay[...] = decay_ref[...]
    inc_state[...] = state_ref[...]
    out_decay[...] = jnp.ones_like(out_decay)
    out_state[...] = jnp.zeros_like(out_state)
    for step, hop in enumerate(hops):
        ahead = place + hop < count
        behind = place >= hop
        inc_buf[step, :, :width] = inc_state[...].astype(jnp.bfloat16)
        inc_buf[step, :, width:] = inc_decay[...].astype(jnp.bfloat16)
        copy = pltpu.make_async_remote_copy(
            src_ref=inc_buf.at[step],
            dst_ref=recv_buf.at[step],
            send_sem=send_sem.at[step],
            recv_sem=recv_sem.at[step],
            device_id=target(jnp.minimum(place + hop, count - 1)),
            device_id_type=pl.DeviceIdType.MESH,
        )

        @pl.when(ahead)
        def _():
            copy.start()

        @pl.when(behind)
        def _():
            copy.wait_recv()
            got_state = recv_buf[step, :, :width].astype(jnp.float32)
            got_decay = recv_buf[step, :, width:].astype(jnp.float32)
            inc_state[...] = inc_decay[:, 0:1] * got_state + inc_state[...]
            inc_decay[...] = got_decay * inc_decay[...]
            out_state[...] = out_decay[:, 0:1] * got_state + out_state[...]
            out_decay[...] = got_decay * out_decay[...]

        @pl.when(ahead)
        def _():
            copy.wait_send()


def entering(decay, state, count):
    heads, rows, width = state.shape
    flat = rows * width
    lanes = 128
    vmem = pl.BlockSpec(memory_space=pltpu.VMEM)
    steps = max(1, (count - 1).bit_length())
    out_decay, out_state = pl.pallas_call(
        functools.partial(scan_kernel, count),
        out_shape=(
            jax.ShapeDtypeStruct((heads, lanes), jnp.float32),
            jax.ShapeDtypeStruct((heads, flat), jnp.float32),
        ),
        in_specs=[vmem, vmem],
        out_specs=(vmem, vmem),
        scratch_shapes=[
            pltpu.VMEM((steps, heads, flat + lanes), jnp.bfloat16),
            pltpu.VMEM((steps, heads, flat + lanes), jnp.bfloat16),
            pltpu.VMEM((heads, lanes), jnp.float32),
            pltpu.VMEM((heads, flat), jnp.float32),
            pltpu.SemaphoreType.DMA((steps,)),
            pltpu.SemaphoreType.DMA((steps,)),
        ],
        compiler_params=pltpu.CompilerParams(collective_id=0, has_side_effects=True),
    )(jnp.broadcast_to(decay[:, None], (heads, lanes)), state.reshape(heads, flat))
    return out_decay[:, 0], out_state.reshape(heads, rows, width)


def route_ranks(quarter_ids, experts):
    flattened = quarter_ids.reshape(-1)
    onehot = (flattened[:, None] == jnp.arange(experts, dtype=jnp.int32)[None, :]).astype(jnp.int32)
    running = jnp.cumsum(onehot, axis=0)
    rank_ids = jnp.sum(onehot * running, axis=1) - 1
    return (flattened, rank_ids)


def place_rows(normed, quarter_ids, experts, capacity):
    flattened, rank_ids = route_ranks(quarter_ids, experts)
    slot_ids = rank_ids * experts + flattened
    matches = (
        jnp.arange(capacity * experts, dtype=jnp.int32)[:, None] == slot_ids[None, :]
    ).astype(jnp.bfloat16)
    doubled = jnp.repeat(normed, quarter_ids.shape[1], axis=0)
    placed = jnp.dot(matches, doubled, preferred_element_type=jnp.float32).astype(jnp.bfloat16)
    return placed.reshape(capacity, experts, normed.shape[1])


def rms_rows(values, gain_vec):
    scaling = lax.rsqrt(jnp.mean(values * values, axis=1, keepdims=True) + eps_norm)
    return (values * scaling * gain_vec[None, :]).astype(jnp.bfloat16)


def local(
    inputs,
    gate_input,
    b_proj,
    c_proj,
    step_size,
    decay_rate,
    skip_gain,
    start_state,
    norm_gain,
    out_proj,
    residual,
    moe_gain,
    w_gate,
    w_up,
    w_down,
    route_ids,
    route_gates,
):
    tok_ctx = inputs.shape[0]
    head_count = step_size.shape[0]
    head_dim = inputs.shape[1] // head_count
    model_width = residual.shape[1]
    n_ctx = lax.axis_size("chip") * lax.axis_size("core")
    n_exp = lax.axis_size("exp")
    experts = n_ctx // PAIR
    tok_quarter = tok_ctx // n_exp
    capacity = 4 * tok_quarter // experts
    x_local = inputs.astype(jnp.float32).reshape(tok_ctx, head_count, head_dim)
    b_local = b_proj.astype(jnp.float32)
    c_local = c_proj.astype(jnp.float32)
    cumulative = jnp.cumsum(decay_rate, axis=1)
    span_total = cumulative[:, -1]
    sequence_indices = jnp.arange(tok_ctx, dtype=jnp.int32)
    causal = sequence_indices[:, None] >= sequence_indices[None, :]
    spread = jnp.where(causal[None], cumulative[:, :, None] - cumulative[:, None, :], 0.0)
    scores = jnp.dot(c_local, b_local.T, precision=top_precision)
    mixing = jnp.where(causal[None], jnp.exp(-spread), 0.0) * scores[None] * step_size[:, None, :]
    inside_part = jnp.einsum("hts,shp->thp", mixing, x_local, precision=top_precision)
    ending = jnp.exp(-(span_total[:, None] - cumulative)) * step_size
    local_state = jnp.einsum("hs,shp,sn->hpn", ending, x_local, b_local, precision=top_precision)
    prior_decay, prior_state = entering(jnp.exp(-span_total), local_state, n_ctx)
    incoming = prior_state + prior_decay[:, None, None] * start_state
    carried = (
        jnp.einsum("hpn,tn->thp", incoming, c_local, precision=top_precision)
        * jnp.exp(-cumulative).T[:, :, None]
    )
    ssm_out = inside_part + carried + skip_gain[None, :, None] * x_local
    gated_out = ssm_out.reshape(tok_ctx, head_count * head_dim) * jax.nn.silu(
        gate_input.astype(jnp.float32)
    )
    squares = jnp.sum(gated_out * gated_out, axis=1)
    unscaled_mix = (gated_out * norm_gain[None, :]).astype(jnp.bfloat16)
    partial_value = jnp.dot(
        unscaled_mix,
        lax.all_gather(out_proj, CTX, axis=1, tiled=True),
        preferred_element_type=jnp.float32,
    )
    width_out = partial_value.shape[1]
    joined = jnp.concatenate(
        [partial_value, jnp.broadcast_to(squares[:, None], (tok_ctx, 128))], axis=1
    ).astype(jnp.bfloat16)
    quarters = lax.all_to_all(
        joined.reshape(n_exp, tok_quarter, joined.shape[1]), "exp", split_axis=0, concat_axis=0, tiled=True
    )
    quarter_sum = jnp.sum(quarters.astype(jnp.float32), axis=0).astype(jnp.bfloat16)
    own_parts = quarter_sum.astype(jnp.float32)
    scaling = lax.rsqrt(own_parts[:, width_out] / (head_count * head_dim * n_exp) + eps_norm)
    mixed_own = own_parts[:, :width_out] * scaling[:, None]
    gate_rows = w_gate[0]
    up_rows = w_up[0]
    down_rows = w_down[0]
    piece_width = gate_rows.shape[1]
    first_row = lax.axis_index("exp") * tok_quarter
    own_ids = lax.dynamic_slice_in_dim(route_ids, first_row, tok_quarter, 0)
    own_gates = lax.dynamic_slice_in_dim(route_gates, first_row, tok_quarter, 0)
    own_residual = lax.dynamic_slice_in_dim(residual, first_row, tok_quarter, 0)
    hidden_own = own_residual.astype(jnp.float32) + mixed_own
    moe_own = rms_rows(hidden_own, moe_gain)
    moe_all = lax.all_to_all(
        jnp.broadcast_to(moe_own[None], (n_exp,) + moe_own.shape), "exp", split_axis=0, concat_axis=0, tiled=True
    ).reshape(tok_ctx, model_width)

    def place_quarter(quarter_rows, quarter_ids):
        return place_rows(quarter_rows, quarter_ids, experts, capacity)

    placed = jax.vmap(place_quarter)(
        moe_all.reshape(n_exp, tok_quarter, model_width),
        route_ids.reshape(n_exp, tok_quarter, route_ids.shape[1]),
    )
    placed = placed.reshape(n_exp * capacity, experts, model_width)
    swap = [(0, 1), (1, 0)]
    mine = lax.all_to_all(placed, "chip", split_axis=1, concat_axis=1, tiled=True)
    other = lax.ppermute(mine, "core", swap)

    def expert_rows(rows, by_permutes):
        flat = rows.reshape(-1, model_width)
        gate_val = jnp.dot(flat, gate_rows, preferred_element_type=jnp.float32)
        up_val = jnp.dot(flat, up_rows, preferred_element_type=jnp.float32)
        activated = (jax.nn.silu(gate_val) * up_val).astype(jnp.bfloat16)
        product = jnp.dot(activated, down_rows, preferred_element_type=jnp.float32)
        pieces = product.astype(jnp.bfloat16).reshape(rows.shape)
        if not by_permutes:
            return lax.psum_scatter(pieces, "exp", scatter_dimension=0, tiled=True)
        split = rows.shape[1] * 3 // 8
        by_call = lax.psum_scatter(pieces[:, :split], "exp", scatter_dimension=0, tiled=True)
        pieces = pieces[:, split:].reshape((n_exp, capacity, rows.shape[1] - split) + rows.shape[2:])
        place = lax.axis_index("exp")
        total = lax.dynamic_index_in_dim(pieces, place, 0, False).astype(jnp.float32)
        for shift in range(1, n_exp):
            outgoing = lax.dynamic_index_in_dim(pieces, (place + shift) % n_exp, 0, False)
            total = total + lax.ppermute(
                outgoing, "exp", [(i, (i + shift) % n_exp) for i in range(n_exp)]
            ).astype(jnp.float32)
        return jnp.concatenate([by_call, total.astype(jnp.bfloat16)], axis=1)

    own_sum = expert_rows(mine, False)
    partner_sum = expert_rows(other, True)
    partner_half = lax.ppermute(partner_sum, "core", swap)
    both_halves = (own_sum.astype(jnp.float32) + partner_half.astype(jnp.float32)).astype(jnp.bfloat16)
    returned = lax.all_to_all(both_halves, "chip", split_axis=1, concat_axis=1, tiled=True)
    flattened, rank_ids = route_ranks(own_ids, experts)
    fetched = returned.reshape(capacity * experts, model_width)[rank_ids * experts + flattened]
    weighted = fetched.astype(jnp.float32) * own_gates.reshape(-1)[:, None]
    moe_out = jnp.sum(weighted.reshape(tok_quarter, -1, model_width), axis=1)
    return (hidden_own + moe_out).astype(jnp.bfloat16)


def solution(mesh):
    in_specs = (
        P(CTX, "exp"),
        P(CTX, "exp"),
        P(CTX, None),
        P(CTX, None),
        P("exp", CTX),
        P("exp", CTX),
        P("exp"),
        P("exp", None, None),
        P("exp"),
        P("exp", CTX),
        P(CTX, None),
        P(),
        P(CTX, None, "exp"),
        P(CTX, None, "exp"),
        P(CTX, "exp", None),
        P(CTX, None),
        P(CTX, None),
    )
    out_specs = P(("chip", "core", "exp"), None)
    split_mesh = Mesh(
        mesh.devices.reshape(mesh.devices.shape[0] // 2, 2, mesh.devices.shape[1]), ("chip", "core", "exp")
    )
    return jax.shard_map(local, mesh=split_mesh, in_specs=in_specs, out_specs=out_specs, check_vma=False)
```
